512 devices in a mesh: seq: 64 (over z, y_lo, core), head: 8 (over y_hi, x).
Axes of the slice: x: 4, y: 8 (y_hi: 2, y_lo: 4; y = y_hi * 4 + y_lo), z: 8, core: 2. Of those that a mesh axis runs over, the one named last changes fastest.
Arguments:
- query: bfloat16 [32768, 32, 128], P('seq', 'head'), may hold values from -6 to 6
- key: bfloat16 [32768, 16, 128], P('seq', 'head'), may hold values from -6 to 6
- value: bfloat16 [32768, 16, 128], P('seq', 'head'), may hold values from -6 to 6
- grad_out: bfloat16 [32768, 32, 128], P('seq', 'head'), may hold values from -25 to 25
- q_gain: float32 [128], replicated, may hold values from 0.1 to 1.9
- k_gain: float32 [128], replicated, may hold values from 0.1 to 1.9
Outputs:
- grad_query: bfloat16 [32768, 32, 128], P('seq', 'head')
- grad_key: bfloat16 [32768, 16, 128], P('seq', 'head')
- grad_value: bfloat16 [32768, 16, 128], P('seq', 'head')
- grad_q_gain: float32 [128], replicated
- grad_k_gain: float32 [128], replicated
The draws below stay inside these ranges and needn't reach their ends.
All inputs are finite; a program needn't handle non-finite values.
Results may differ from the reference program's by a relative error of at most 0.0099.
Values may be sent and summed in bfloat16 or wider, within the bound.
A program may use at most 64 MiB of HBM per device.

```python
import jax
import jax.numpy as jnp
from jax import lax

QUERY_HEADS = 32
KEY_VALUE_HEADS = 16
HEAD_SIZE = 128
WINDOW = 1024
TOKENS_PER_SHARD = 512
DOCUMENT_TOKENS = 32768


def draw_grad_out(key, part):
    first_key = jax.random.fold_in(jax.random.fold_in(key, 7), 0)
    array_shape = (DOCUMENT_TOKENS, QUERY_HEADS, HEAD_SIZE)
    ramp_pos = jnp.arange(DOCUMENT_TOKENS, dtype=jnp.float32) / (DOCUMENT_TOKENS - 1)
    ramp_scale = jnp.power(3.0, ramp_pos)
    base_part = jnp.clip(jax.random.normal(first_key, array_shape, jnp.float32), -4.0, 4.0)
    return (base_part * ramp_scale[:, None, None]).astype(jnp.bfloat16)


def shard_levels(stream_key, shape, pieces, low, largest):
    factor_of = 1.0
    for position, blocks in pieces:
        heights = jax.random.uniform(jax.random.fold_in(jax.random.fold_in(stream_key, 6), position), (blocks,), jnp.float32, low / len(pieces), largest / len(pieces))
        factor_of = factor_of * jnp.repeat(jnp.exp(heights), shape[position] // blocks).reshape((-1,) + (1,) * (len(shape) - 1 - position))
    return factor_of


def gaussian(own_key, extent, scale, most, shards=(), held_as=jnp.bfloat16):
    array = scale * jax.random.normal(own_key, extent, jnp.float32)
    if shards:
        array = array * shard_levels(own_key, extent, shards, -0.22, 0.18)
    return jnp.clip(array, -most, most).astype(held_as)


def setup_inputs(seed: int = 0) -> dict:
    key_list = jax.random.split(jax.random.key(seed), 7)
    query = gaussian(key_list[0], (DOCUMENT_TOKENS, QUERY_HEADS, HEAD_SIZE), 1.0, 6.0, ((0, 64), (1, 8)))
    key = gaussian(key_list[1], (DOCUMENT_TOKENS, KEY_VALUE_HEADS, HEAD_SIZE), 1.0, 6.0, ((0, 64), (1, 8)))
    value = gaussian(key_list[2], (DOCUMENT_TOKENS, KEY_VALUE_HEADS, HEAD_SIZE), 1.0, 6.0, ((0, 64), (1, 8)))
    grad_out = draw_grad_out(jax.random.fold_in(key_list[6], 71), 0)
    q_gain = jnp.clip(1.0 + 0.18 * jax.random.normal(key_list[4], (HEAD_SIZE,), jnp.float32), 0.1, 1.9)
    k_gain = jnp.clip(1.0 + 0.18 * jax.random.normal(key_list[5], (HEAD_SIZE,), jnp.float32), 0.1, 1.9)
    return {"query": query, "key": key, "value": value, "grad_out": grad_out, "q_gain": q_gain, "k_gain": k_gain}


score_scale = 168.0 ** (-0.5)
norm_eps = 1e-06

def normalize(inputs_raw, gain_vec):
    as_float = inputs_raw.astype(jnp.float32)
    inverse_rms = lax.rsqrt(lax.optimization_barrier(jnp.mean(as_float * as_float, axis=-1, keepdims=True)) + norm_eps)
    unit_rows = as_float * inverse_rms
    return (unit_rows * gain_vec, unit_rows, inverse_rms)

def norm_back(d_normed, unit_rows, inverse_rms, gain_vec):
    d_unit = d_normed * gain_vec
    d_inputs = inverse_rms * (d_unit - unit_rows * lax.optimization_barrier(jnp.mean(d_unit * unit_rows, axis=-1, keepdims=True)))
    d_gain = lax.optimization_barrier(jnp.sum(d_normed * unit_rows, axis=(0, 1)))
    return (d_inputs, d_gain)

def reference(query, key, value, grad_out, q_gain, k_gain):
    reach_total = (WINDOW + TOKENS_PER_SHARD - 1) // TOKENS_PER_SHARD
    key_span = (reach_total + 1) * TOKENS_PER_SHARD
    heads_per_group = QUERY_HEADS // KEY_VALUE_HEADS
    q_normed, q_unit, q_inverse = normalize(query, q_gain)
    k_normed, k_unit, k_inverse = normalize(key, k_gain)
    query_low = q_normed.astype(jnp.bfloat16)
    key_low = k_normed.astype(jnp.bfloat16)
    pad_amount = jnp.zeros((reach_total * TOKENS_PER_SHARD, KEY_VALUE_HEADS, HEAD_SIZE), jnp.bfloat16)
    key_pad = jnp.concatenate([pad_amount, key_low], axis=0)
    value_pad = jnp.concatenate([pad_amount, value], axis=0)
    row_ids = jnp.arange(TOKENS_PER_SHARD, dtype=jnp.int32)[:, None]
    col_ids = jnp.arange(key_span, dtype=jnp.int32)[None, :]
    distance_grid = row_ids + reach_total * TOKENS_PER_SHARD - col_ids
    base_allowed = (distance_grid >= 0) & (distance_grid < WINDOW)

    def block_step(totals, block_id):
        key_total, value_total = totals
        start_row = block_id * TOKENS_PER_SHARD
        query_block = lax.dynamic_slice_in_dim(query_low, start_row, TOKENS_PER_SHARD, 0)
        incoming_gradient = lax.dynamic_slice_in_dim(grad_out, start_row, TOKENS_PER_SHARD, 0)
        key_blk = lax.dynamic_slice_in_dim(key_pad, start_row, key_span, 0)
        value_blk = lax.dynamic_slice_in_dim(value_pad, start_row, key_span, 0)
        allowed = base_allowed & (col_ids + start_row >= reach_total * TOKENS_PER_SHARD)
        query_float32 = query_block.reshape(TOKENS_PER_SHARD, KEY_VALUE_HEADS, heads_per_group, HEAD_SIZE).astype(jnp.float32)
        incoming_gradient_float32 = incoming_gradient.reshape(TOKENS_PER_SHARD, KEY_VALUE_HEADS, heads_per_group, HEAD_SIZE).astype(jnp.float32)
        key_f32 = key_blk.astype(jnp.float32)
        value_f32 = value_blk.astype(jnp.float32)
        scores = score_scale * jnp.einsum('tkgd,skd->kgts', query_float32, key_f32)
        exp_scores = jnp.where(allowed[None, None], jnp.exp(scores), 0.0)
        attn_probs = exp_scores / lax.optimization_barrier(jnp.sum(exp_scores, axis=-1, keepdims=True))
        probs_low = lax.optimization_barrier(attn_probs.astype(jnp.bfloat16)).astype(jnp.float32)
        attended = jnp.einsum('kgts,skd->tkgd', probs_low, value_f32)
        offset = jnp.einsum('tkgd,tkgd->kgt', incoming_gradient_float32, attended)[..., None]
        d_probs = jnp.einsum('tkgd,skd->kgts', incoming_gradient_float32, value_f32)
        d_scores = lax.optimization_barrier((attn_probs * (d_probs - offset)).astype(jnp.bfloat16)).astype(jnp.float32)
        value_grad = jnp.einsum('kgts,tkgd->skd', probs_low, incoming_gradient_float32)
        query_grad = score_scale * jnp.einsum('kgts,skd->tkgd', d_scores, key_f32)
        key_grad = score_scale * jnp.einsum('kgts,tkgd->skd', d_scores, query_float32)
        key_total = lax.dynamic_update_slice_in_dim(key_total, lax.dynamic_slice_in_dim(key_total, start_row, key_span, 0) + key_grad, start_row, 0)
        value_total = lax.dynamic_update_slice_in_dim(value_total, lax.dynamic_slice_in_dim(value_total, start_row, key_span, 0) + value_grad, start_row, 0)
        return ((key_total, value_total), query_grad.reshape(TOKENS_PER_SHARD, QUERY_HEADS, HEAD_SIZE))
    blank_array = jnp.zeros((DOCUMENT_TOKENS + reach_total * TOKENS_PER_SHARD, KEY_VALUE_HEADS, HEAD_SIZE), jnp.float32)
    (key_total, value_total), query_parts = lax.scan(block_step, (blank_array, blank_array), jnp.arange(DOCUMENT_TOKENS // TOKENS_PER_SHARD, dtype=jnp.int32))
    query_grad_n = query_parts.reshape(DOCUMENT_TOKENS, QUERY_HEADS, HEAD_SIZE)
    key_grad_n = key_total[reach_total * TOKENS_PER_SHARD:]
    grad_value = value_total[reach_total * TOKENS_PER_SHARD:].astype(jnp.bfloat16)
    grad_query, grad_q_gain = norm_back(query_grad_n, q_unit, q_inverse, q_gain)
    grad_key, grad_k_gain = norm_back(key_grad_n, k_unit, k_inverse, k_gain)
    return (grad_query.astype(jnp.bfloat16), grad_key.astype(jnp.bfloat16), grad_value, grad_q_gain, grad_k_gain)
```

```python
import functools
import math

import jax
import jax.numpy as jnp
from jax import lax
from jax.experimental import pallas as pl
from jax.experimental.pallas import tpu as pltpu
from jax.sharding import PartitionSpec as P

WINDOW = 1024
SCALE = 168.0 ** (-0.5)
EXP2_SCALE = SCALE * math.log2(math.e)
EPS = 1e-06
CORES = 2
Y_LO = 4
Y_HI = 2

BF = jnp.bfloat16
F32 = jnp.float32
MESH = pl.DeviceIdType.MESH

T = 512
D = 128
B = 256
KEYS = 3 * T
EXT = 16


def dot_nn(a, b):
    return lax.dot_general(a, b, (((1,), (0,)), ((), ())), preferred_element_type=F32)


def dot_nt(a, b):
    return lax.dot_general(a, b, (((1,), (1,)), ((), ())), preferred_element_type=F32)


def transposed(x):
    return jnp.transpose(x.astype(F32)).astype(BF)


def kernel(
    sizes,
    q_in, k_in, v_in, g_in, q_gain, k_gain,
    gq_out, gk_out, gv_out, gain_out,
    q_buf, g_buf, k_buf, v_buf,
    q_unit, q_inv, k_unit, k_inv, stage,
    q_ext, q_low, g_t, g_ext,
    kv, v_ok, v_t, k_t, e_s, ds_s, av_s, dq_t,
    dk_s, dv_s, dq_s,
    send_b, recv_b, send_r, recv_r,
    red_src, red_y, red_z, red_x,
    in_sem, out_sem,
    f_send, f_recv, s_send, s_recv, b_send, b_recv, r_send, r_recv,
    ys_sem, yr_sem, zs_sem, zr_sem, xs_sem, xr_sem,
):
    n_seq, n_head = sizes
    n_z = n_seq // (CORES * Y_LO)
    n_x = n_head // Y_HI
    seq = lax.axis_index("seq")
    head = lax.axis_index("head")
    core = lax.rem(seq, CORES)
    y_lo = lax.rem(lax.div(seq, CORES), Y_LO)
    z = lax.div(seq, CORES * Y_LO)
    x = lax.rem(head, n_x)
    y_hi = lax.div(head, n_x)
    ahead = (lax.rem(seq + 2, n_seq), head)
    behind = (lax.rem(seq + n_seq - 2, n_seq), head)
    sibling = (seq + 1 - 2 * core, head)
    is_odd = core == 1
    is_even = core == 0

    n_y = Y_HI * Y_LO * CORES
    y_rank = (y_hi * Y_LO + y_lo) * CORES + core

    def y_peer(d):
        r = lax.rem(y_rank + d, n_y)
        c = lax.rem(r, CORES)
        yl = lax.rem(lax.div(r, CORES), Y_LO)
        yh = lax.div(r, CORES * Y_LO)
        return ((z * Y_LO + yl) * CORES + c, yh * n_x + x)

    def z_peer(d):
        return ((lax.rem(z + d, n_z) * Y_LO + y_lo) * CORES + core, head)

    def x_peer(d):
        return (seq, y_hi * n_x + lax.rem(x + d, n_x))

    peers = [ahead, behind, sibling]
    peers += [y_peer(d) for d in range(1, n_y)]
    peers += [z_peer(d) for d in range(1, n_z)]
    peers += [x_peer(d) for d in range(1, n_x)]

    ins = [
        pltpu.make_async_copy(src, dst, in_sem.at[i])
        for i, (src, dst) in enumerate(
            ((k_in, k_buf), (v_in, v_buf), (q_in, q_buf), (g_in, g_buf))
        )
    ]
    for c in ins:
        c.start()
    barrier = pltpu.get_barrier_semaphore()
    for p in peers:
        pl.semaphore_signal(barrier, inc=1, device_id=p, device_id_type=MESH)

    ok = [
        (seq >= 2).astype(F32),
        (seq >= 1).astype(F32),
        jnp.float32(1.0),
    ]

    def normalise(buf, unit, inv, rows):
        for r in range(0, rows, B):
            f = buf[r : r + B, :].astype(F32)
            i = lax.rsqrt(jnp.mean(f * f, axis=1, keepdims=True) + EPS)
            unit[r : r + B, :] = f * i
            inv[r : r + B, :] = jnp.broadcast_to(i, (B, D))

    kg = k_gain[...]
    qg = q_gain[...]
    ins[0].wait()
    normalise(k_buf, k_unit, k_inv, 2 * T)
    ins[1].wait()
    stage[: 2 * T, :] = v_buf[...].astype(F32)
    for kh in range(2):
        kv[2, kh, 0] = (k_unit[pl.ds(kh, T, stride=2), :] * kg).astype(BF)
        kv[2, kh, 1] = stage[pl.ds(kh, T, stride=2), :].astype(BF)
    pl.semaphore_wait(barrier, len(peers))

    def remote(src, dst, ssem, rsem, dev):
        return pltpu.make_async_remote_copy(
            src_ref=src, dst_ref=dst, send_sem=ssem, recv_sem=rsem, device_id=dev, device_id_type=MESH
        )

    fwd = [remote(kv.at[2, kh], kv.at[0, kh], f_send.at[kh], f_recv.at[kh], ahead) for kh in range(2)]
    sib_own = [remote(kv.at[2, kh], kv.at[1, kh], s_send.at[kh], s_recv.at[kh], sibling) for kh in range(2)]
    sib_fwd = [remote(kv.at[0, kh], kv.at[1, kh], s_send.at[kh], s_recv.at[kh], sibling) for kh in range(2)]
    ret_b = [remote(send_b.at[kh], recv_b.at[kh], b_send.at[kh], b_recv.at[kh], sibling) for kh in range(2)]
    ret_r = [remote(send_r.at[kh], recv_r.at[kh], r_send.at[kh], r_recv.at[kh], behind) for kh in range(2)]

    for kh in range(2):
        fwd[kh].start()

        @pl.when(is_even)
        def _(kh=kh):
            sib_own[kh].start()

    ins[2].wait()
    normalise(q_buf, q_unit, q_inv, 4 * T)
    ins[3].wait()
    stage[...] = g_buf[...].astype(F32)
    for kh in range(2):
        for qb in range(2):
            for h in range(2):
                rows = pl.ds(4 * B * qb + 2 * kh + h, B, stride=4)
                low = (q_unit[rows, :] * qg).astype(BF)
                scaled = low.astype(F32) * EXP2_SCALE
                high = scaled.astype(BF)
                rest = (scaled - high.astype(F32)).astype(BF)
                at = slice(h * B, (h + 1) * B)
                q_low[kh, qb, at, :] = low
                q_ext[kh, qb, at, :D] = high
                q_ext[kh, qb, at, D:] = rest
                g_t[kh, qb, :, at] = jnp.transpose(stage[rows, :]).astype(BF)

    def prepare(sh, kh):
        value = (kv[sh, kh, 1].astype(F32) * ok[sh]).astype(BF)
        span = slice(sh * T, (sh + 1) * T)
        v_ok[kh, span, :] = value
        v_t[kh, :D, span] = transposed(value)
        v_t[kh, D:, span] = jnp.full((EXT, T), ok[sh], F32).astype(BF)
        k_t[kh, :, span] = transposed(kv[sh, kh, 0])

    key_row = lax.broadcasted_iota(jnp.int32, (B, 2 * B), 0)
    query_col = lax.rem(lax.broadcasted_iota(jnp.int32, (B, 2 * B), 1), B)

    def pass1(kh, qb, r0, r1, first):
        off = qb * B
        for b in range(r0, r1, B):
            k = kv[b // T, kh, 0, b % T : b % T + B, :]
            s = dot_nt(jnp.concatenate([k, k], axis=1), q_ext[kh, qb])
            e = jnp.exp2(s)
            if b == off:
                e = jnp.where(key_row > query_col, e, 0.0)
            if b == off + WINDOW:
                e = jnp.where(key_row <= query_col, e, 0.0)
            e_s[kh, qb, b - off : b - off + B, :] = e.astype(BF)
        av = dot_nn(v_t[kh, :, r0:r1], e_s[kh, qb, r0 - off : r1 - off, :])
        if first:
            av_s[kh, qb] = av
        else:
            av_s[kh, qb] += av

    def finish(kh, qb):
        l_row = av_s[kh, qb, D : D + 1, :]
        inv = 1.0 / l_row
        scaled = (g_t[kh, qb].astype(F32) * inv).astype(BF)
        g_ext[kh, qb, :D, :] = scaled
        off = -inv * jnp.sum(scaled.astype(F32) * av_s[kh, qb, :D, :], axis=0, keepdims=True)
        high = off.astype(BF).astype(F32)
        rest = off - high
        row = lax.broadcasted_iota(jnp.int32, (EXT, 2 * B), 0)
        tail = jnp.where(row == 0, high, jnp.where(row == 1, rest, 0.0))
        g_ext[kh, qb, D : D + EXT, :] = tail.astype(BF)
        g_ext[kh, qb, D + EXT :, :] = jnp.zeros((D - EXT, 2 * B), BF)

    def pass2(kh, qb, r0, r1, first_q, first_of):
        off = qb * B
        for b in range(r0, r1, B):
            sh = b // T
            ones = jnp.full((B, D), ok[sh], F32).astype(BF)
            vx = jnp.concatenate([v_ok[kh, b : b + B, :], ones], axis=1)
            dp = dot_nn(vx, g_ext[kh, qb])
            e = e_s[kh, qb, b - off : b - off + B, :]
            ds = e * dp.astype(BF)
            ds_s[b - off : b - off + B, :] = ds
            dv = dot_nt(e, g_ext[kh, qb, :D, :])
            dk = dot_nn(ds, q_low[kh, qb])
            if first_of(b):
                dv_s[kh, b : b + B, :] = dv
                dk_s[kh, b : b + B, :] = dk
            else:
                dv_s[kh, b : b + B, :] += dv
                dk_s[kh, b : b + B, :] += dk
        dq = dot_nn(k_t[kh, :, r0:r1], ds_s[r0 - off : r1 - off, :])
        if first_q:
            dq_t[kh, qb] = dq
        else:
            dq_t[kh, qb] += dq

    for kh in range(2):
        prepare(2, kh)
        pass1(kh, 0, 2 * T, 2 * T + B, True)
        pass1(kh, 1, 2 * T, 3 * T, True)

    odd_f = is_odd.astype(F32)
    even_f = is_even.astype(F32)

    for kh in range(2):
        fwd[kh].wait_recv()

        @pl.when(is_odd)
        def _(kh=kh):
            sib_fwd[kh].start()

        prepare(0, kh)
        sib_own[kh].wait_recv()
        prepare(1, kh)
        pass1(kh, 0, 0, 2 * T, False)
        pass1(kh, 1, B, 2 * T, False)
        finish(kh, 0)
        finish(kh, 1)
        pass2(kh, 0, 0, 2 * T, True, lambda b: True)
        pass2(kh, 1, B, 2 * T, True, lambda b: False)
        send_b[kh, 0] = (dk_s[kh, T : 2 * T, :] * (SCALE * ok[1])).astype(BF)
        send_b[kh, 1] = (dv_s[kh, T : 2 * T, :] * ok[1]).astype(BF)
        ret_b[kh].start()
        pass2(kh, 0, 2 * T, 2 * T + B, False, lambda b: True)
        pass2(kh, 1, 2 * T, 3 * T, False, lambda b: b >= 2 * T + B)
        ret_b[kh].wait_recv()
        send_r[kh, 0] = (dk_s[kh, :T, :] * (SCALE * ok[0]) + recv_b[kh, 0].astype(F32) * odd_f).astype(BF)
        send_r[kh, 1] = (dv_s[kh, :T, :] * ok[0] + recv_b[kh, 1].astype(F32) * odd_f).astype(BF)
        ret_r[kh].start()

    k_sum = jnp.zeros((8, D), F32)
    for kh in range(2):
        for sh in range(3):
            prod = dk_s[kh, sh * T : (sh + 1) * T, :] * kv[sh, kh, 0].astype(F32)
            k_sum = k_sum + jnp.sum(prod.reshape(T // 8, 8, D), axis=0)
    k_sum = jnp.sum(k_sum, axis=0, keepdims=True) * (SCALE / kg)
    for kh in range(2):
        for qb in range(2):
            for h in range(2):
                rows = pl.ds(4 * B * qb + 2 * kh + h, B, stride=4)
                dq_s[rows, :] = jnp.transpose(dq_t[kh, qb, :, h * B : (h + 1) * B]) * SCALE
    q_sum = jnp.sum((dq_s[...] * q_unit[...]).reshape(4 * T // 8, 8, D), axis=0)
    q_sum = jnp.sum(q_sum, axis=0, keepdims=True)
    row8 = lax.broadcasted_iota(jnp.int32, (8, D), 0)
    red_src[0] = jnp.where(row8 == 0, q_sum, jnp.where(row8 == 1, k_sum, 0.0))

    def exchange(level, dst, ssem, rsem, peer, count):
        copies = [
            remote(red_src.at[level], dst.at[d - 1], ssem.at[d - 1], rsem.at[d - 1], peer(d))
            for d in range(1, count)
        ]
        for c in copies:
            c.start()
        return copies

    def absorb(level, dst, copies):
        for c in copies:
            c.wait_recv()
        total = red_src[level]
        for d in range(len(copies)):
            total = total + dst[d]
        red_src[level + 1] = total

    y_copies = exchange(0, red_y, ys_sem, yr_sem, y_peer, n_y)

    def norm_back(grad, unit, inv, gain, out_buf, rows):
        for r in range(0, rows, B):
            u = unit[r : r + B, :]
            du = grad[r : r + B, :] * gain
            m = jnp.mean(du * u, axis=1, keepdims=True)
            out_buf[r : r + B, :] = (inv[r : r + B, :] * (du - u * m)).astype(BF)

    norm_back(dq_s, q_unit, q_inv, qg, q_buf, 4 * T)
    out_q = pltpu.make_async_copy(q_buf, gq_out, out_sem.at[0])
    out_q.start()
    absorb(0, red_y, y_copies)
    z_copies = exchange(1, red_z, zs_sem, zr_sem, z_peer, n_z)

    for kh in range(2):
        ret_r[kh].wait_recv()
        rows = pl.ds(kh, T, stride=2)
        dq_s[rows, :] = (
            dk_s[kh, 2 * T :, :] * SCALE
            + recv_r[kh, 0].astype(F32)
            + recv_b[kh, 0].astype(F32) * even_f
        )
        stage[rows, :] = (
            dv_s[kh, 2 * T :, :] + recv_r[kh, 1].astype(F32) + recv_b[kh, 1].astype(F32) * even_f
        )
    norm_back(dq_s, k_unit, k_inv, kg, k_buf, 2 * T)
    out_k = pltpu.make_async_copy(k_buf, gk_out, out_sem.at[1])
    out_k.start()
    v_buf[...] = stage[: 2 * T, :].astype(BF)
    out_v = pltpu.make_async_copy(v_buf, gv_out, out_sem.at[2])
    out_v.start()
    absorb(1, red_z, z_copies)
    x_copies = exchange(2, red_x, xs_sem, xr_sem, x_peer, n_x)
    absorb(2, red_x, x_copies)
    gain_out[...] = red_src[3]

    for c in y_copies + z_copies + x_copies:
        c.wait_send()
    for kh in range(2):
        fwd[kh].wait_send()
        sib_own[kh].wait_send()
        ret_b[kh].wait_send()
        ret_r[kh].wait_send()
    out_q.wait()
    out_k.wait()
    out_v.wait()


def per_device(n_seq, n_head, query, key, value, grad_out, q_gain, k_gain):
    n_y = Y_HI * Y_LO * CORES
    n_z = n_seq // (CORES * Y_LO)
    n_x = n_head // Y_HI
    hbm = pl.BlockSpec(memory_space=pl.ANY)
    vmem = pl.BlockSpec(memory_space=pltpu.VMEM)
    dma = pltpu.SemaphoreType.DMA
    scratch = [
        pltpu.VMEM((4 * T, D), BF), pltpu.VMEM((4 * T, D), BF),
        pltpu.VMEM((2 * T, D), BF), pltpu.VMEM((2 * T, D), BF),
        pltpu.VMEM((4 * T, D), F32), pltpu.VMEM((4 * T, D), F32),
        pltpu.VMEM((2 * T, D), F32), pltpu.VMEM((2 * T, D), F32),
        pltpu.VMEM((4 * T, D), F32),
        pltpu.VMEM((2, 2, 2 * B, 2 * D), BF), pltpu.VMEM((2, 2, 2 * B, D), BF),
        pltpu.VMEM((2, 2, D, 2 * B), BF), pltpu.VMEM((2, 2, 2 * D, 2 * B), BF),
        pltpu.VMEM((3, 2, 2, T, D), BF),
        pltpu.VMEM((2, KEYS, D), BF),
        pltpu.VMEM((2, D + EXT, KEYS), BF),
        pltpu.VMEM((2, D, KEYS), BF),
        pltpu.VMEM((2, 2, WINDOW + B, 2 * B), BF),
        pltpu.VMEM((WINDOW + B, 2 * B), BF),
        pltpu.VMEM((2, 2, D + EXT, 2 * B), F32),
        pltpu.VMEM((2, 2, D, 2 * B), F32),
        pltpu.VMEM((2, KEYS, D), F32), pltpu.VMEM((2, KEYS, D), F32),
        pltpu.VMEM((4 * T, D), F32),
        pltpu.VMEM((2, 2, T, D), BF), pltpu.VMEM((2, 2, T, D), BF),
        pltpu.VMEM((2, 2, T, D), BF), pltpu.VMEM((2, 2, T, D), BF),
        pltpu.VMEM((4, 8, D), F32),
        pltpu.VMEM((n_y - 1, 8, D), F32),
        pltpu.VMEM((max(n_z - 1, 1), 8, D), F32),
        pltpu.VMEM((max(n_x - 1, 1), 8, D), F32),
        dma((4,)), dma((3,)),
        dma((2,)), dma((2,)), dma((2,)), dma((2,)), dma((2,)), dma((2,)), dma((2,)), dma((2,)),
        dma((n_y - 1,)), dma((n_y - 1,)),
        dma((max(n_z - 1, 1),)), dma((max(n_z - 1, 1),)),
        dma((max(n_x - 1, 1),)), dma((max(n_x - 1, 1),)),
    ]
    gq, gk, gv, gains = pl.pallas_call(
        functools.partial(kernel, (n_seq, n_head)),
        out_shape=(
            jax.ShapeDtypeStruct((4 * T, D), BF),
            jax.ShapeDtypeStruct((2 * T, D), BF),
            jax.ShapeDtypeStruct((2 * T, D), BF),
            jax.ShapeDtypeStruct((8, D), F32),
        ),
        in_specs=[hbm] * 4 + [vmem] * 2,
        out_specs=(hbm, hbm, hbm, vmem),
        scratch_shapes=scratch,
        compiler_params=pltpu.CompilerParams(collective_id=0, has_side_effects=True),
        name="swa_backward",
    )(
        query.reshape(4 * T, D),
        key.reshape(2 * T, D),
        value.reshape(2 * T, D),
        grad_out.reshape(4 * T, D),
        q_gain.reshape(1, D),
        k_gain.reshape(1, D),
    )
    return (
        gq.reshape(T, 4, D),
        gk.reshape(T, 2, D),
        gv.reshape(T, 2, D),
        gains[0],
        gains[1],
    )


def solution(mesh):
    split = P("seq", "head", None)
    return jax.shard_map(
        functools.partial(per_device, mesh.shape["seq"], mesh.shape["head"]),
        mesh=mesh,
        in_specs=(split, split, split, split, P(), P()),
        out_specs=(split, split, split, P(), P()),
        check_vma=False,
    )
```

```python
import functools
import math

import jax
import jax.numpy as jnp
from jax import lax
from jax.experimental import pallas as pl
from jax.experimental.pallas import tpu as pltpu
from jax.sharding import PartitionSpec as P

WINDOW = 1024
SCALE = 168.0 ** (-0.5)
EXP2_SCALE = SCALE * math.log2(math.e)
EPS = 1e-06
CORES = 2
Y_LO = 4
Y_HI = 2

BF = jnp.bfloat16
F32 = jnp.float32
MESH = pl.DeviceIdType.MESH

T = 512
D = 128
B = 256
KEYS = 3 * T
EXT = 16


def dot_nn(a, b):
    return lax.dot_general(a, b, (((1,), (0,)), ((), ())), preferred_element_type=F32)


def dot_nt(a, b):
    return lax.dot_general(a, b, (((1,), (1,)), ((), ())), preferred_element_type=F32)


def transposed(x):
    return jnp.transpose(x.astype(F32)).astype(BF)


def kernel(
    sizes,
    q_in, k_in, v_in, g_in, q_gain, k_gain,
    gq_out, gk_out, gv_out, gq_gain_out, gk_gain_out,
    q_buf, g_buf, k_buf, v_buf,
    q_unit, q_inv, k_unit, k_inv, stage,
    q_ext, q_low, g_t, g_ext,
    kv, v_t, k_t, e_s, ds_s, av_s, dq_t,
    dk_s, dv_s, dq_s,
    send_b, recv_b, send_r, recv_r,
    red_src, red_y, red_z, red_x,
    in_sem, up_sem, down_sem,
    f_send, f_recv, s_send, s_recv, b_send, b_recv, r_send, r_recv,
    ys_sem, yr_sem, zs_sem, zr_sem, xs_sem, xr_sem,
):
    n_seq, n_head = sizes
    n_z = n_seq // (CORES * Y_LO)
    n_x = n_head // Y_HI
    n_y = Y_HI * Y_LO * CORES
    seq = lax.axis_index("seq")
    head = lax.axis_index("head")
    core = lax.rem(seq, CORES)
    y_lo = lax.rem(lax.div(seq, CORES), Y_LO)
    z = lax.div(seq, CORES * Y_LO)
    x = lax.rem(head, n_x)
    y_hi = lax.div(head, n_x)
    y_rank = (y_hi * Y_LO + y_lo) * CORES + core
    ahead = (seq + 2, head)
    behind = (seq - 2, head)
    sibling = (seq + 1 - 2 * core, head)
    z_step = CORES * Y_LO
    above = (seq + z_step, head)
    below = (seq - z_step, head)
    is_odd = core == 1
    is_even = core == 0
    has_ahead = seq < n_seq - 2
    has_behind = seq >= 2
    has_above = z < n_z - 1
    has_below = z > 0

    def y_peer(d):
        r = lax.rem(y_rank + d, n_y)
        c = lax.rem(r, CORES)
        yl = lax.rem(lax.div(r, CORES), Y_LO)
        yh = lax.div(r, CORES * Y_LO)
        return ((z * Y_LO + yl) * CORES + c, yh * n_x + x)

    def z_peer(d):
        return ((lax.rem(z + d, n_z) * Y_LO + y_lo) * CORES + core, head)

    def x_peer(d):
        return (seq, y_hi * n_x + lax.rem(x + d, n_x))

    def signal(sem, dev):
        pl.semaphore_signal(sem, inc=1, device_id=dev, device_id_type=MESH)

    def remote(src, dst, ssem, rsem, dev):
        return pltpu.make_async_remote_copy(
            src_ref=src, dst_ref=dst, send_sem=ssem, recv_sem=rsem, device_id=dev, device_id_type=MESH
        )

    ins = [
        pltpu.make_async_copy(src, dst, in_sem.at[i])
        for i, (src, dst) in enumerate(
            ((k_in, k_buf), (v_in, v_buf), (q_in, q_buf), (g_in, g_buf))
        )
    ]
    for c in ins:
        c.start()

    barrier = pltpu.get_barrier_semaphore()
    always = [y_peer(d) for d in range(1, n_y)] + [x_peer(d) for d in range(1, n_x)]
    for p in always:
        signal(barrier, p)
    sometimes = ((has_ahead, ahead), (has_behind, behind), (has_above, above), (has_below, below))
    expected = jnp.int32(len(always))
    for there, p in sometimes:
        expected = expected + there.astype(jnp.int32)

        @pl.when(there)
        def _(p=p):
            signal(barrier, p)

    ok = [has_behind.astype(F32), (seq >= 1).astype(F32), jnp.float32(1.0)]

    @pl.when(jnp.logical_not(has_behind))
    def _():
        kv[0] = jnp.zeros((2, 2, T, D), BF)

    @pl.when(seq == 0)
    def _():
        kv[1] = jnp.zeros((2, 2, T, D), BF)

    @pl.when(jnp.logical_not(has_ahead))
    def _():
        recv_r[...] = jnp.zeros((2, 2, T, D), BF)

    def normalise(buf, unit, inv, rows):
        for r in range(0, rows, B):
            f = buf[r : r + B, :].astype(F32)
            i = lax.rsqrt(jnp.mean(f * f, axis=1, keepdims=True) + EPS)
            unit[r : r + B, :] = f * i
            inv[r : r + B, :] = jnp.broadcast_to(i, (B, D))

    kg = k_gain[...]
    qg = q_gain[...]
    ins[0].wait()
    normalise(k_buf, k_unit, k_inv, 2 * T)
    ins[1].wait()
    stage[: 2 * T, :] = v_buf[...].astype(F32)
    for kh in range(2):
        kv[2, kh, 0] = (k_unit[pl.ds(kh, T, stride=2), :] * kg).astype(BF)
        kv[2, kh, 1] = stage[pl.ds(kh, T, stride=2), :].astype(BF)
    pl.semaphore_wait(barrier, expected)

    parts = [(kh, i) for kh in range(2) for i in range(2)]
    fwd = {p: remote(kv.at[2, *p], kv.at[0, *p], f_send.at[*p], f_recv.at[*p], ahead) for p in parts}
    sib_own = {p: remote(kv.at[2, *p], kv.at[1, *p], s_send.at[*p], s_recv.at[*p], sibling) for p in parts}
    sib_fwd = {p: remote(kv.at[0, *p], kv.at[1, *p], s_send.at[*p], s_recv.at[*p], sibling) for p in parts}
    ret_b = [remote(send_b.at[kh], recv_b.at[kh], b_send.at[kh], b_recv.at[kh], sibling) for kh in range(2)]
    ret_r = [remote(send_r.at[kh], recv_r.at[kh], r_send.at[kh], r_recv.at[kh], behind) for kh in range(2)]

    @pl.when(has_ahead)
    def _():
        for p in parts:
            fwd[p].start()

    @pl.when(is_even)
    def _():
        for p in parts:
            sib_own[p].start()

    @pl.when(jnp.logical_not(has_below))
    def _():
        signal(up_sem, above)

    @pl.when(jnp.logical_not(has_above))
    def _():
        signal(down_sem, below)

    def pass_up():
        @pl.when(has_below)
        def _():
            pl.semaphore_wait(up_sem, 1)

            @pl.when(has_above)
            def _():
                signal(up_sem, above)

    def pass_down(low, high):
        @pl.when(has_above & (z >= low) & (z < high))
        def _():
            pl.semaphore_wait(down_sem, 1)

            @pl.when(has_below)
            def _():
                signal(down_sem, below)

    def rows_of(kh, qb, h):
        return pl.ds(4 * B * qb + 2 * kh + h, B, stride=4)

    ins[2].wait()
    normalise(q_buf, q_unit, q_inv, 4 * T)
    ins[3].wait()
    stage[...] = g_buf[...].astype(F32)
    for kh in range(2):
        for qb in range(2):
            for h in range(2):
                rows = rows_of(kh, qb, h)
                low = (q_unit[rows, :] * qg).astype(BF)
                scaled = low.astype(F32) * EXP2_SCALE
                high = scaled.astype(BF)
                rest = (scaled - high.astype(F32)).astype(BF)
                at = slice(h * B, (h + 1) * B)
                q_low[kh, qb, at, :] = low
                q_ext[kh, qb, at, :D] = high
                q_ext[kh, qb, at, D:] = rest
                g_t[kh, qb, :, at] = jnp.transpose(stage[rows, :]).astype(BF)
    pass_up()
    pass_down(n_z - 3, n_z)

    def prepare_k(sh, kh):
        k_t[kh, :, sh * T : (sh + 1) * T] = transposed(kv[sh, kh, 0])

    def prepare_v(sh, kh):
        span = slice(sh * T, (sh + 1) * T)
        v_t[kh, :D, span] = transposed(kv[sh, kh, 1])
        v_t[kh, D:, span] = jnp.full((EXT, T), ok[sh], F32).astype(BF)

    key_row = lax.broadcasted_iota(jnp.int32, (B, 2 * B), 0)
    query_col = lax.rem(lax.broadcasted_iota(jnp.int32, (B, 2 * B), 1), B)

    def weigh(kh, qb, r0, r1):
        off = qb * B
        for b in range(r0, r1, B):
            k = kv[b // T, kh, 0, b % T : b % T + B, :]
            s = dot_nt(jnp.concatenate([k, k], axis=1), q_ext[kh, qb])
            e = jnp.exp2(s)
            if b == off:
                e = jnp.where(key_row > query_col, e, 0.0)
            if b == off + WINDOW:
                e = jnp.where(key_row <= query_col, e, 0.0)
            e_s[kh, qb, b - off : b - off + B, :] = e.astype(BF)

    def attend(kh, qb, r0, r1, first):
        off = qb * B
        av = dot_nn(v_t[kh, :, r0:r1], e_s[kh, qb, r0 - off : r1 - off, :])
        if first:
            av_s[kh, qb] = av
        else:
            av_s[kh, qb] += av

    def finish(kh, qb):
        l_row = av_s[kh, qb, D : D + 1, :]
        inv = 1.0 / l_row
        scaled = (g_t[kh, qb].astype(F32) * inv).astype(BF)
        g_ext[kh, qb, :D, :] = scaled
        off = -inv * jnp.sum(scaled.astype(F32) * av_s[kh, qb, :D, :], axis=0, keepdims=True)
        high = off.astype(BF).astype(F32)
        rest = off - high
        row = lax.broadcasted_iota(jnp.int32, (EXT, 2 * B), 0)
        tail = jnp.where(row == 0, high, jnp.where(row == 1, rest, 0.0))
        g_ext[kh, qb, D : D + EXT, :] = tail.astype(BF)
        g_ext[kh, qb, D + EXT :, :] = jnp.zeros((D - EXT, 2 * B), BF)

    def grads(kh, qb, r0, r1, first_q, first_of):
        off = qb * B
        for b in range(r0, r1, B):
            sh = b // T
            ones = jnp.full((B, D), ok[sh], F32).astype(BF)
            vx = jnp.concatenate([kv[sh, kh, 1, b % T : b % T + B, :], ones], axis=1)
            dp = dot_nn(vx, g_ext[kh, qb])
            e = e_s[kh, qb, b - off : b - off + B, :]
            ds = e * dp.astype(BF)
            ds_s[b - off : b - off + B, :] = ds
            dv = dot_nt(e, g_ext[kh, qb, :D, :])
            dk = dot_nn(ds, q_low[kh, qb])
            if first_of(b):
                dv_s[kh, b : b + B, :] = dv
                dk_s[kh, b : b + B, :] = dk
            else:
                dv_s[kh, b : b + B, :] += dv
                dk_s[kh, b : b + B, :] += dk
        dq = dot_nn(k_t[kh, :, r0:r1], ds_s[r0 - off : r1 - off, :])
        if first_q:
            dq_t[kh, qb] = dq
        else:
            dq_t[kh, qb] += dq

    for kh in range(2):
        prepare_k(2, kh)
        weigh(kh, 0, 2 * T, 2 * T + B)
        weigh(kh, 1, 2 * T, 3 * T)
    for kh in range(2):
        prepare_v(2, kh)
        attend(kh, 0, 2 * T, 2 * T + B, True)
        attend(kh, 1, 2 * T, 3 * T, True)

    odd_f = is_odd.astype(F32)
    even_f = is_even.astype(F32)

    def take(p):
        @pl.when(has_behind)
        def _():
            fwd[p].wait_recv()

            @pl.when(is_odd)
            def _():
                sib_fwd[p].start()

    def take_b(p):
        @pl.when(seq >= 1)
        def _():
            sib_own[p].wait_recv()

    def pay_back(kh):
        ret_b[kh].wait_recv()
        send_r[kh, 0] = (dk_s[kh, :T, :] * SCALE + recv_b[kh, 0].astype(F32) * odd_f).astype(BF)
        send_r[kh, 1] = (dv_s[kh, :T, :] + recv_b[kh, 1].astype(F32) * odd_f).astype(BF)

        @pl.when(has_behind)
        def _():
            ret_r[kh].start()

    q_sum = jnp.zeros((8, D), F32)
    k_sum = jnp.zeros((8, D), F32)
    for kh in range(2):
        if kh == 0:
            take((0, 0))
        prepare_k(0, kh)
        take_b((kh, 0))
        prepare_k(1, kh)
        weigh(kh, 0, 0, 2 * T)
        weigh(kh, 1, B, 2 * T)
        take((kh, 1))
        prepare_v(0, kh)
        take_b((kh, 1))
        prepare_v(1, kh)
        attend(kh, 0, 0, 2 * T, False)
        attend(kh, 1, B, 2 * T, False)
        finish(kh, 0)
        finish(kh, 1)
        grads(kh, 0, 0, 2 * T, True, lambda b: True)
        grads(kh, 1, B, 2 * T, True, lambda b: False)
        send_b[kh, 0] = (dk_s[kh, T : 2 * T, :] * SCALE).astype(BF)
        send_b[kh, 1] = dv_s[kh, T : 2 * T, :].astype(BF)
        ret_b[kh].start()
        if kh == 0:
            take((1, 0))
        grads(kh, 0, 2 * T, 2 * T + B, False, lambda b: True)
        grads(kh, 1, 2 * T, 3 * T, False, lambda b: b >= 2 * T + B)
        for sh in range(3):
            prod = dk_s[kh, sh * T : (sh + 1) * T, :] * kv[sh, kh, 0].astype(F32)
            k_sum = k_sum + jnp.sum(prod.reshape(T // 8, 8, D), axis=0)
        for qb in range(2):
            for h in range(2):
                rows = rows_of(kh, qb, h)
                dq = jnp.transpose(dq_t[kh, qb, :, h * B : (h + 1) * B]) * SCALE
                dq_s[rows, :] = dq
                q_sum = q_sum + jnp.sum((dq * q_unit[rows, :]).reshape(B // 8, 8, D), axis=0)
        if kh == 0:
            pay_back(0)
            pass_down(n_z - 5, n_z - 3)
    pass_down(0, n_z - 5)

    k_row = jnp.sum(k_sum, axis=0, keepdims=True) * (SCALE / kg)
    q_row = jnp.sum(q_sum, axis=0, keepdims=True)
    row8 = lax.broadcasted_iota(jnp.int32, (8, D), 0)
    red_src[0] = jnp.where(row8 == 0, q_row, jnp.where(row8 == 1, k_row, 0.0))

    def exchange(level, dst, ssem, rsem, peer, count):
        copies = [
            remote(red_src.at[level], dst.at[d - 1], ssem.at[d - 1], rsem.at[d - 1], peer(d))
            for d in range(1, count)
        ]
        for c in copies:
            c.start()
        return copies

    def absorb(level, dst, copies):
        for c in copies:
            c.wait_recv()
        total = red_src[level]
        for d in range(len(copies)):
            total = total + dst[d]
        red_src[level + 1] = total

    y_copies = exchange(0, red_y, ys_sem, yr_sem, y_peer, n_y)
    pay_back(1)

    def norm_back(grad, unit, inv, gain, out, rows):
        for r in range(0, rows, B):
            u = unit[r : r + B, :]
            du = grad[r : r + B, :] * gain
            m = jnp.mean(du * u, axis=1, keepdims=True)
            out[r : r + B, :] = (inv[r : r + B, :] * (du - u * m)).astype(BF)

    absorb(0, red_y, y_copies)
    z_copies = exchange(1, red_z, zs_sem, zr_sem, z_peer, n_z)
    norm_back(dq_s, q_unit, q_inv, qg, gq_out, 4 * T)
    absorb(1, red_z, z_copies)
    x_copies = exchange(2, red_x, xs_sem, xr_sem, x_peer, n_x)

    for kh in range(2):

        @pl.when(has_ahead)
        def _(kh=kh):
            ret_r[kh].wait_recv()

        rows = pl.ds(kh, T, stride=2)
        dq_s[rows, :] = (
            dk_s[kh, 2 * T :, :] * SCALE
            + recv_r[kh, 0].astype(F32)
            + recv_b[kh, 0].astype(F32) * even_f
        )
        stage[rows, :] = (
            dv_s[kh, 2 * T :, :] + recv_r[kh, 1].astype(F32) + recv_b[kh, 1].astype(F32) * even_f
        )
    norm_back(dq_s, k_unit, k_inv, kg, gk_out, 2 * T)
    gv_out[...] = stage[: 2 * T, :].astype(BF)
    absorb(2, red_x, x_copies)
    gq_gain_out[...] = red_src[3, 0:1, :]
    gk_gain_out[...] = red_src[3, 1:2, :]

    for c in y_copies + z_copies + x_copies + ret_b:
        c.wait_send()

    @pl.when(has_ahead)
    def _():
        for p in parts:
            fwd[p].wait_send()

    @pl.when(is_even | has_behind)
    def _():
        for p in parts:
            sib_own[p].wait_send()

    @pl.when(has_behind)
    def _():
        for kh in range(2):
            ret_r[kh].wait_send()


def write_out(*refs):
    sem = refs[-1]
    n = (len(refs) - 1) // 2
    copies = [pltpu.make_async_copy(refs[i], refs[n + i], sem.at[i]) for i in range(n)]
    for c in copies:
        c.start()
    for c in copies:
        c.wait()


def per_device(n_seq, n_head, query, key, value, grad_out, q_gain, k_gain):
    n_y = Y_HI * Y_LO * CORES
    n_z = n_seq // (CORES * Y_LO)
    n_x = n_head // Y_HI
    hbm = pl.BlockSpec(memory_space=pl.ANY)
    vmem = pl.BlockSpec(memory_space=pltpu.VMEM)
    dma = pltpu.SemaphoreType.DMA
    scratch = [
        pltpu.VMEM((4 * T, D), BF), pltpu.VMEM((4 * T, D), BF),
        pltpu.VMEM((2 * T, D), BF), pltpu.VMEM((2 * T, D), BF),
        pltpu.VMEM((4 * T, D), F32), pltpu.VMEM((4 * T, D), F32),
        pltpu.VMEM((2 * T, D), F32), pltpu.VMEM((2 * T, D), F32),
        pltpu.VMEM((4 * T, D), F32),
        pltpu.VMEM((2, 2, 2 * B, 2 * D), BF), pltpu.VMEM((2, 2, 2 * B, D), BF),
        pltpu.VMEM((2, 2, D, 2 * B), BF), pltpu.VMEM((2, 2, 2 * D, 2 * B), BF),
        pltpu.VMEM((3, 2, 2, T, D), BF),
        pltpu.VMEM((2, D + EXT, KEYS), BF),
        pltpu.VMEM((2, D, KEYS), BF),
        pltpu.VMEM((2, 2, WINDOW + B, 2 * B), BF),
        pltpu.VMEM((WINDOW + B, 2 * B), BF),
        pltpu.VMEM((2, 2, D + EXT, 2 * B), F32),
        pltpu.VMEM((2, 2, D, 2 * B), F32),
        pltpu.VMEM((2, KEYS, D), F32), pltpu.VMEM((2, KEYS, D), F32),
        pltpu.VMEM((4 * T, D), F32),
        pltpu.VMEM((2, 2, T, D), BF), pltpu.VMEM((2, 2, T, D), BF),
        pltpu.VMEM((2, 2, T, D), BF), pltpu.VMEM((2, 2, T, D), BF),
        pltpu.VMEM((4, 8, D), F32),
        pltpu.VMEM((n_y - 1, 8, D), F32),
        pltpu.VMEM((max(n_z - 1, 1), 8, D), F32),
        pltpu.VMEM((max(n_x - 1, 1), 8, D), F32),
        dma((4,)), pltpu.SemaphoreType.REGULAR, pltpu.SemaphoreType.REGULAR,
        dma((2, 2)), dma((2, 2)), dma((2, 2)), dma((2, 2)), dma((2,)), dma((2,)), dma((2,)), dma((2,)),
        dma((n_y - 1,)), dma((n_y - 1,)),
        dma((max(n_z - 1, 1),)), dma((max(n_z - 1, 1),)),
        dma((max(n_x - 1, 1),)), dma((max(n_x - 1, 1),)),
    ]
    shapes = [((4 * T, D), BF), ((2 * T, D), BF), ((2 * T, D), BF), ((1, D), F32), ((1, D), F32)]
    held = pl.pallas_call(
        functools.partial(kernel, (n_seq, n_head)),
        out_shape=[pltpu.VMEM(*s) for s in shapes],
        in_specs=[hbm] * 4 + [vmem] * 2,
        out_specs=[vmem] * len(shapes),
        scratch_shapes=scratch,
        compiler_params=pltpu.CompilerParams(collective_id=0, has_side_effects=True),
        name="swa_backward",
    )(
        query.reshape(4 * T, D),
        key.reshape(2 * T, D),
        value.reshape(2 * T, D),
        grad_out.reshape(4 * T, D),
        q_gain.reshape(1, D),
        k_gain.reshape(1, D),
    )
    gq, gk, gv, gq_gain, gk_gain = pl.pallas_call(
        write_out,
        out_shape=[jax.ShapeDtypeStruct(*s) for s in shapes],
        in_specs=[vmem] * len(shapes),
        out_specs=[hbm] * len(shapes),
        scratch_shapes=[dma((len(shapes),))],
        name="write_out",
    )(*[pltpu.with_memory_space_constraint(a, pltpu.VMEM) for a in held])
    return (
        gq.reshape(T, 4, D),
        gk.reshape(T, 2, D),
        gv.reshape(T, 2, D),
        gq_gain.reshape(D),
        gk_gain.reshape(D),
    )


def solution(mesh):
    split = P("seq", "head", None)
    return jax.shard_map(
        functools.partial(per_device, mesh.shape["seq"], mesh.shape["head"]),
        mesh=mesh,
        in_specs=(split, split, split, split, P(), P()),
        out_specs=(split, split, split, P(), P()),
        check_vma=False,
    )
```

```python
import functools
import math

import jax
import jax.numpy as jnp
from jax import lax
from jax.experimental import pallas as pl
from jax.experimental.pallas import tpu as pltpu
from jax.sharding import PartitionSpec as P

WINDOW = 1024
SCALE = 168.0 ** (-0.5)
EXP2_SCALE = SCALE * math.log2(math.e)
EPS = 1e-06
CORES = 2
Y_LO = 4
Y_HI = 2

BF = jnp.bfloat16
F32 = jnp.float32
MESH = pl.DeviceIdType.MESH

T = 512
D = 128
B = 256
KEYS = 3 * T
EXT = 16


def dot_nn(a, b):
    return lax.dot_general(a, b, (((1,), (0,)), ((), ())), preferred_element_type=F32)


def dot_nt(a, b):
    return lax.dot_general(a, b, (((1,), (1,)), ((), ())), preferred_element_type=F32)


def transposed(x):
    return jnp.transpose(x.astype(F32)).astype(BF)


def kernel(
    sizes,
    q_in, k_in, v_in, g_in, q_gain, k_gain,
    gq_out, gk_out, gv_out, gq_gain_out, gk_gain_out,
    q_buf, g_buf, k_buf, v_buf,
    q_unit, q_inv, k_unit, k_inv, stage,
    q_ext, q_low, g_t, g_ext,
    k_raw, kv, v_t, k_t, e_s, ds_s, av_s, dq_t,
    dk_s, dv_s, dq_s,
    send_b, recv_b, send_r, recv_r,
    red_src, red_y, red_z, red_x,
    in_sem, up_sem, down_sem,
    f_send, f_recv, s_send, s_recv, b_send, b_recv, r_send, r_recv,
    ys_sem, yr_sem, zs_sem, zr_sem, xs_sem, xr_sem,
):
    n_seq, n_head = sizes
    n_z = n_seq // (CORES * Y_LO)
    n_x = n_head // Y_HI
    n_y = Y_HI * Y_LO * CORES
    seq = lax.axis_index("seq")
    head = lax.axis_index("head")
    core = lax.rem(seq, CORES)
    y_lo = lax.rem(lax.div(seq, CORES), Y_LO)
    z = lax.div(seq, CORES * Y_LO)
    x = lax.rem(head, n_x)
    y_hi = lax.div(head, n_x)
    y_rank = (y_hi * Y_LO + y_lo) * CORES + core
    ahead = (seq + 2, head)
    behind = (seq - 2, head)
    sibling = (seq + 1 - 2 * core, head)
    z_step = CORES * Y_LO
    above = (seq + z_step, head)
    below = (seq - z_step, head)
    is_odd = core == 1
    is_even = core == 0
    has_ahead = seq < n_seq - 2
    has_behind = seq >= 2
    has_above = z < n_z - 1
    has_below = z > 0

    def y_peer(d):
        r = lax.rem(y_rank + d, n_y)
        c = lax.rem(r, CORES)
        yl = lax.rem(lax.div(r, CORES), Y_LO)
        yh = lax.div(r, CORES * Y_LO)
        return ((z * Y_LO + yl) * CORES + c, yh * n_x + x)

    def z_peer(d):
        return ((lax.rem(z + d, n_z) * Y_LO + y_lo) * CORES + core, head)

    def x_peer(d):
        return (seq, y_hi * n_x + lax.rem(x + d, n_x))

    def signal(sem, dev):
        pl.semaphore_signal(sem, inc=1, device_id=dev, device_id_type=MESH)

    def remote(src, dst, ssem, rsem, dev):
        return pltpu.make_async_remote_copy(
            src_ref=src, dst_ref=dst, send_sem=ssem, recv_sem=rsem, device_id=dev, device_id_type=MESH
        )

    ins = [
        pltpu.make_async_copy(src, dst, in_sem.at[i])
        for i, (src, dst) in enumerate(
            ((k_in, k_buf), (v_in, v_buf), (q_in, q_buf), (g_in, g_buf))
        )
    ]
    for c in ins:
        c.start()

    barrier = pltpu.get_barrier_semaphore()
    always = [y_peer(d) for d in range(1, n_y)] + [x_peer(d) for d in range(1, n_x)]
    for p in always:
        signal(barrier, p)
    sometimes = ((has_ahead, ahead), (has_behind, behind), (has_above, above), (has_below, below))
    expected = jnp.int32(len(always))
    for there, p in sometimes:
        expected = expected + there.astype(jnp.int32)

        @pl.when(there)
        def _(p=p):
            signal(barrier, p)

    ok = [has_behind.astype(F32), (seq >= 1).astype(F32), jnp.float32(1.0)]

    @pl.when(jnp.logical_not(has_behind))
    def _():
        k_raw[0] = jnp.zeros((2 * T, D), BF)
        kv[0] = jnp.zeros((2, 2, T, D), BF)

    @pl.when(seq == 0)
    def _():
        k_raw[1] = jnp.zeros((2 * T, D), BF)
        kv[1] = jnp.zeros((2, 2, T, D), BF)

    @pl.when(jnp.logical_not(has_ahead))
    def _():
        recv_r[...] = jnp.zeros((2, 2, T, D), BF)

    def normalise(buf, unit, inv, rows):
        for r in range(0, rows, B):
            f = buf[r : r + B, :].astype(F32)
            i = lax.rsqrt(jnp.mean(f * f, axis=1, keepdims=True) + EPS)
            unit[r : r + B, :] = f * i
            inv[r : r + B, :] = jnp.broadcast_to(i, (B, D))

    kg = k_gain[...]
    qg = q_gain[...]
    def pieces(sh, own):
        return [k_in if own else k_raw.at[sh]] + [kv.at[2 if own else sh, kh, 1] for kh in range(2)]

    def hop(own, sh, ssem, rsem, dev):
        return [
            remote(src, dst, ssem.at[i], rsem.at[i], dev)
            for i, (src, dst) in enumerate(zip(pieces(0, own), pieces(sh, False)))
        ]

    fwd = hop(True, 0, f_send, f_recv, ahead)
    sib_own = hop(True, 1, s_send, s_recv, sibling)
    sib_fwd = hop(False, 1, s_send, s_recv, sibling)
    ret_b = [remote(send_b.at[kh], recv_b.at[kh], b_send.at[kh], b_recv.at[kh], sibling) for kh in range(2)]
    ret_r = [remote(send_r.at[kh], recv_r.at[kh], r_send.at[kh], r_recv.at[kh], behind) for kh in range(2)]

    def give(i):
        @pl.when(has_ahead)
        def _():
            fwd[i].start()

        @pl.when(is_even)
        def _():
            sib_own[i].start()

    pl.semaphore_wait(barrier, expected)
    give(0)
    ins[1].wait()
    stage[: 2 * T, :] = v_buf[...].astype(F32)
    for kh in range(2):
        kv[2, kh, 1] = stage[pl.ds(kh, T, stride=2), :].astype(BF)
    give(1)
    give(2)

    @pl.when(jnp.logical_not(has_below))
    def _():
        signal(up_sem, above)

    @pl.when(jnp.logical_not(has_above))
    def _():
        signal(down_sem, below)

    def pass_up():
        @pl.when(has_below)
        def _():
            pl.semaphore_wait(up_sem, 1)

            @pl.when(has_above)
            def _():
                signal(up_sem, above)

    def pass_down(low, high):
        @pl.when(has_above & (z >= low) & (z < high))
        def _():
            pl.semaphore_wait(down_sem, 1)

            @pl.when(has_below)
            def _():
                signal(down_sem, below)

    def rows_of(kh, qb, h):
        return pl.ds(4 * B * qb + 2 * kh + h, B, stride=4)

    ins[0].wait()
    normalise(k_buf, k_unit, k_inv, 2 * T)
    for kh in range(2):
        kv[2, kh, 0] = (k_unit[pl.ds(kh, T, stride=2), :] * kg).astype(BF)
    ins[2].wait()
    normalise(q_buf, q_unit, q_inv, 4 * T)
    ins[3].wait()
    stage[...] = g_buf[...].astype(F32)
    for kh in range(2):
        for qb in range(2):
            for h in range(2):
                rows = rows_of(kh, qb, h)
                low = (q_unit[rows, :] * qg).astype(BF)
                scaled = low.astype(F32) * EXP2_SCALE
                high = scaled.astype(BF)
                rest = (scaled - high.astype(F32)).astype(BF)
                at = slice(h * B, (h + 1) * B)
                q_low[kh, qb, at, :] = low
                q_ext[kh, qb, at, :D] = high
                q_ext[kh, qb, at, D:] = rest
                g_t[kh, qb, :, at] = jnp.transpose(stage[rows, :]).astype(BF)
    pass_up()
    pass_down(n_z - 3, n_z)

    def prepare_k(sh):
        if sh < 2:
            for r in range(0, 2 * T, B):
                f = k_raw[sh, r : r + B, :].astype(F32)
                i = lax.rsqrt(jnp.mean(f * f, axis=1, keepdims=True) + EPS)
                stage[r : r + B, :] = f * i * kg
        for kh in range(2):
            if sh < 2:
                kv[sh, kh, 0] = stage[pl.ds(kh, T, stride=2), :].astype(BF)
            k_t[kh, :, sh * T : (sh + 1) * T] = transposed(kv[sh, kh, 0])

    def prepare_v(sh, kh):
        span = slice(sh * T, (sh + 1) * T)
        v_t[kh, :D, span] = transposed(kv[sh, kh, 1])
        v_t[kh, D:, span] = jnp.full((EXT, T), ok[sh], F32).astype(BF)

    key_row = lax.broadcasted_iota(jnp.int32, (B, 2 * B), 0)
    query_col = lax.rem(lax.broadcasted_iota(jnp.int32, (B, 2 * B), 1), B)

    def weigh(kh, qb, r0, r1):
        off = qb * B
        for b in range(r0, r1, B):
            k = kv[b // T, kh, 0, b % T : b % T + B, :]
            s = dot_nt(jnp.concatenate([k, k], axis=1), q_ext[kh, qb])
            e = jnp.exp2(s)
            if b == off:
                e = jnp.where(key_row > query_col, e, 0.0)
            if b == off + WINDOW:
                e = jnp.where(key_row <= query_col, e, 0.0)
            e_s[kh, qb, b - off : b - off + B, :] = e.astype(BF)

    def attend(kh, qb, r0, r1, first):
        off = qb * B
        av = dot_nn(v_t[kh, :, r0:r1], e_s[kh, qb, r0 - off : r1 - off, :])
        if first:
            av_s[kh, qb] = av
        else:
            av_s[kh, qb] += av

    def finish(kh, qb):
        l_row = av_s[kh, qb, D : D + 1, :]
        inv = 1.0 / l_row
        scaled = (g_t[kh, qb].astype(F32) * inv).astype(BF)
        g_ext[kh, qb, :D, :] = scaled
        off = -inv * jnp.sum(scaled.astype(F32) * av_s[kh, qb, :D, :], axis=0, keepdims=True)
        high = off.astype(BF).astype(F32)
        rest = off - high
        row = lax.broadcasted_iota(jnp.int32, (EXT, 2 * B), 0)
        tail = jnp.where(row == 0, high, jnp.where(row == 1, rest, 0.0))
        g_ext[kh, qb, D : D + EXT, :] = tail.astype(BF)
        g_ext[kh, qb, D + EXT :, :] = jnp.zeros((D - EXT, 2 * B), BF)

    def grads(kh, qb, r0, r1, first_q, first_of):
        off = qb * B
        for b in range(r0, r1, B):
            sh = b // T
            ones = jnp.full((B, D), ok[sh], F32).astype(BF)
            vx = jnp.concatenate([kv[sh, kh, 1, b % T : b % T + B, :], ones], axis=1)
            dp = dot_nn(vx, g_ext[kh, qb])
            e = e_s[kh, qb, b - off : b - off + B, :]
            ds = e * dp.astype(BF)
            ds_s[b - off : b - off + B, :] = ds
            dv = dot_nt(e, g_ext[kh, qb, :D, :])
            dk = dot_nn(ds, q_low[kh, qb])
            if first_of(b):
                dv_s[kh, b : b + B, :] = dv
                dk_s[kh, b : b + B, :] = dk
            else:
                dv_s[kh, b : b + B, :] += dv
                dk_s[kh, b : b + B, :] += dk
        dq = dot_nn(k_t[kh, :, r0:r1], ds_s[r0 - off : r1 - off, :])
        if first_q:
            dq_t[kh, qb] = dq
        else:
            dq_t[kh, qb] += dq

    prepare_k(2)
    for kh in range(2):
        weigh(kh, 0, 2 * T, 2 * T + B)
        weigh(kh, 1, 2 * T, 3 * T)
    for kh in range(2):
        prepare_v(2, kh)
        attend(kh, 0, 2 * T, 2 * T + B, True)
        attend(kh, 1, 2 * T, 3 * T, True)

    odd_f = is_odd.astype(F32)
    even_f = is_even.astype(F32)

    def take(p):
        @pl.when(has_behind)
        def _():
            fwd[p].wait_recv()

            @pl.when(is_odd)
            def _():
                sib_fwd[p].start()

    def take_b(p):
        @pl.when(seq >= 1)
        def _():
            sib_own[p].wait_recv()

    def pay_back(kh):
        ret_b[kh].wait_recv()
        send_r[kh, 0] = (dk_s[kh, :T, :] * SCALE + recv_b[kh, 0].astype(F32) * odd_f).astype(BF)
        send_r[kh, 1] = (dv_s[kh, :T, :] + recv_b[kh, 1].astype(F32) * odd_f).astype(BF)

        @pl.when(has_behind)
        def _():
            ret_r[kh].start()

    take(0)
    prepare_k(0)
    take_b(0)
    prepare_k(1)
    for kh in range(2):
        weigh(kh, 0, 0, 2 * T)
        weigh(kh, 1, B, 2 * T)

    q_sum = jnp.zeros((8, D), F32)
    k_sum = jnp.zeros((8, D), F32)
    for kh in range(2):
        if kh == 0:
            take(1)
        prepare_v(0, kh)
        take_b(1 + kh)
        prepare_v(1, kh)
        attend(kh, 0, 0, 2 * T, False)
        attend(kh, 1, B, 2 * T, False)
        finish(kh, 0)
        finish(kh, 1)
        grads(kh, 0, 0, 2 * T, True, lambda b: True)
        grads(kh, 1, B, 2 * T, True, lambda b: False)
        send_b[kh, 0] = (dk_s[kh, T : 2 * T, :] * SCALE).astype(BF)
        send_b[kh, 1] = dv_s[kh, T : 2 * T, :].astype(BF)
        ret_b[kh].start()
        if kh == 0:
            take(2)
        grads(kh, 0, 2 * T, 2 * T + B, False, lambda b: True)
        grads(kh, 1, 2 * T, 3 * T, False, lambda b: b >= 2 * T + B)
        for sh in range(3):
            prod = dk_s[kh, sh * T : (sh + 1) * T, :] * kv[sh, kh, 0].astype(F32)
            k_sum = k_sum + jnp.sum(prod.reshape(T // 8, 8, D), axis=0)
        for qb in range(2):
            for h in range(2):
                rows = rows_of(kh, qb, h)
                dq = jnp.transpose(dq_t[kh, qb, :, h * B : (h + 1) * B]) * SCALE
                dq_s[rows, :] = dq
                q_sum = q_sum + jnp.sum((dq * q_unit[rows, :]).reshape(B // 8, 8, D), axis=0)
        if kh == 0:
            pay_back(0)
            pass_down(n_z - 5, n_z - 3)
    pass_down(0, n_z - 5)

    k_row = jnp.sum(k_sum, axis=0, keepdims=True) * (SCALE / kg)
    q_row = jnp.sum(q_sum, axis=0, keepdims=True)
    red_src[0] = jnp.concatenate([q_row, k_row], axis=0)

    def exchange(level, dst, ssem, rsem, peer, count):
        copies = [
            remote(red_src.at[level], dst.at[d - 1], ssem.at[d - 1], rsem.at[d - 1], peer(d))
            for d in range(1, count)
        ]
        for c in copies:
            c.start()
        return copies

    def absorb(level, dst, copies):
        for c in copies:
            c.wait_recv()
        total = red_src[level]
        for d in range(len(copies)):
            total = total + dst[d]
        red_src[level + 1] = total

    def norm_back(grad, unit, inv, gain, out, rows):
        for r in range(0, rows, B):
            u = unit[r : r + B, :]
            du = grad[r : r + B, :] * gain
            m = jnp.mean(du * u, axis=1, keepdims=True)
            out[r : r + B, :] = (inv[r : r + B, :] * (du - u * m)).astype(BF)

    z_copies = exchange(0, red_z, zs_sem, zr_sem, z_peer, n_z)
    pay_back(1)
    norm_back(dq_s, q_unit, q_inv, qg, gq_out, 4 * T)
    absorb(0, red_z, z_copies)
    x_copies = exchange(1, red_x, xs_sem, xr_sem, x_peer, n_x)
    absorb(1, red_x, x_copies)
    y_copies = exchange(2, red_y, ys_sem, yr_sem, y_peer, n_y)

    for kh in range(2):

        @pl.when(has_ahead)
        def _(kh=kh):
            ret_r[kh].wait_recv()

        rows = pl.ds(kh, T, stride=2)
        dq_s[rows, :] = (
            dk_s[kh, 2 * T :, :] * SCALE
            + recv_r[kh, 0].astype(F32)
            + recv_b[kh, 0].astype(F32) * even_f
        )
        stage[rows, :] = (
            dv_s[kh, 2 * T :, :] + recv_r[kh, 1].astype(F32) + recv_b[kh, 1].astype(F32) * even_f
        )
    norm_back(dq_s, k_unit, k_inv, kg, gk_out, 2 * T)
    gv_out[...] = stage[: 2 * T, :].astype(BF)
    absorb(2, red_y, y_copies)
    gq_gain_out[...] = red_src[3, 0:1, :]
    gk_gain_out[...] = red_src[3, 1:2, :]

    for c in y_copies + z_copies + x_copies + ret_b:
        c.wait_send()

    @pl.when(has_ahead)
    def _():
        for c in fwd:
            c.wait_send()

    @pl.when(is_even | has_behind)
    def _():
        for c in sib_own:
            c.wait_send()

    @pl.when(has_behind)
    def _():
        for kh in range(2):
            ret_r[kh].wait_send()


def write_out(*refs):
    sem = refs[-1]
    n = (len(refs) - 1) // 2
    copies = [pltpu.make_async_copy(refs[i], refs[n + i], sem.at[i]) for i in range(n)]
    for c in copies:
        c.start()
    for c in copies:
        c.wait()


def per_device(n_seq, n_head, query, key, value, grad_out, q_gain, k_gain):
    n_y = Y_HI * Y_LO * CORES
    n_z = n_seq // (CORES * Y_LO)
    n_x = n_head // Y_HI
    hbm = pl.BlockSpec(memory_space=pl.ANY)
    vmem = pl.BlockSpec(memory_space=pltpu.VMEM)
    dma = pltpu.SemaphoreType.DMA
    scratch = [
        pltpu.VMEM((4 * T, D), BF), pltpu.VMEM((4 * T, D), BF),
        pltpu.VMEM((2 * T, D), BF), pltpu.VMEM((2 * T, D), BF),
        pltpu.VMEM((4 * T, D), F32), pltpu.VMEM((4 * T, D), F32),
        pltpu.VMEM((2 * T, D), F32), pltpu.VMEM((2 * T, D), F32),
        pltpu.VMEM((4 * T, D), F32),
        pltpu.VMEM((2, 2, 2 * B, 2 * D), BF), pltpu.VMEM((2, 2, 2 * B, D), BF),
        pltpu.VMEM((2, 2, D, 2 * B), BF), pltpu.VMEM((2, 2, 2 * D, 2 * B), BF),
        pltpu.VMEM((2, 2 * T, D), BF),
        pltpu.VMEM((3, 2, 2, T, D), BF),
        pltpu.VMEM((2, D + EXT, KEYS), BF),
        pltpu.VMEM((2, D, KEYS), BF),
        pltpu.VMEM((2, 2, WINDOW + B, 2 * B), BF),
        pltpu.VMEM((WINDOW + B, 2 * B), BF),
        pltpu.VMEM((2, 2, D + EXT, 2 * B), F32),
        pltpu.VMEM((2, 2, D, 2 * B), F32),
        pltpu.VMEM((2, KEYS, D), F32), pltpu.VMEM((2, KEYS, D), F32),
        pltpu.VMEM((4 * T, D), F32),
        pltpu.VMEM((2, 2, T, D), BF), pltpu.VMEM((2, 2, T, D), BF),
        pltpu.VMEM((2, 2, T, D), BF), pltpu.VMEM((2, 2, T, D), BF),
        pltpu.VMEM((4, 2, D), F32),
        pltpu.VMEM((n_y - 1, 2, D), F32),
        pltpu.VMEM((max(n_z - 1, 1), 2, D), F32),
        pltpu.VMEM((max(n_x - 1, 1), 2, D), F32),
        dma((4,)), pltpu.SemaphoreType.REGULAR, pltpu.SemaphoreType.REGULAR,
        dma((3,)), dma((3,)), dma((3,)), dma((3,)), dma((2,)), dma((2,)), dma((2,)), dma((2,)),
        dma((n_y - 1,)), dma((n_y - 1,)),
        dma((max(n_z - 1, 1),)), dma((max(n_z - 1, 1),)),
        dma((max(n_x - 1, 1),)), dma((max(n_x - 1, 1),)),
    ]
    shapes = [((4 * T, D), BF), ((2 * T, D), BF), ((2 * T, D), BF), ((1, D), F32), ((1, D), F32)]
    held = pl.pallas_call(
        functools.partial(kernel, (n_seq, n_head)),
        out_shape=[pltpu.VMEM(*s) for s in shapes],
        in_specs=[hbm] * 4 + [vmem] * 2,
        out_specs=[vmem] * len(shapes),
        scratch_shapes=scratch,
        compiler_params=pltpu.CompilerParams(collective_id=0, has_side_effects=True),
        name="swa_backward",
    )(
        query.reshape(4 * T, D),
        key.reshape(2 * T, D),
        value.reshape(2 * T, D),
        grad_out.reshape(4 * T, D),
        q_gain.reshape(1, D),
        k_gain.reshape(1, D),
    )
    gq, gk, gv, gq_gain, gk_gain = pl.pallas_call(
        write_out,
        out_shape=[jax.ShapeDtypeStruct(*s) for s in shapes],
        in_specs=[vmem] * len(shapes),
        out_specs=[hbm] * len(shapes),
        scratch_shapes=[dma((len(shapes),))],
        name="write_out",
    )(*[pltpu.with_memory_space_constraint(a, pltpu.VMEM) for a in held])
    return (
        gq.reshape(T, 4, D),
        gk.reshape(T, 2, D),
        gv.reshape(T, 2, D),
        gq_gain.reshape(D),
        gk_gain.reshape(D),
    )


def solution(mesh):
    split = P("seq", "head", None)
    return jax.shard_map(
        functools.partial(per_device, mesh.shape["seq"], mesh.shape["head"]),
        mesh=mesh,
        in_specs=(split, split, split, split, P(), P()),
        out_specs=(split, split, split, P(), P()),
        check_vma=False,
    )
```

```python
import functools
import math

import jax
import jax.numpy as jnp
from jax import lax
from jax.experimental import pallas as pl
from jax.experimental.pallas import tpu as pltpu
from jax.sharding import PartitionSpec as P

WINDOW = 1024
SCALE = 168.0 ** (-0.5)
EXP2_SCALE = SCALE * math.log2(math.e)
EPS = 1e-06
CORES = 2
Y_LO = 4
Y_HI = 2

BF = jnp.bfloat16
F32 = jnp.float32
MESH = pl.DeviceIdType.MESH

T = 512
D = 128
B = 256
KEYS = 3 * T
EXT = 16


def dot_nn(a, b):
    return lax.dot_general(a, b, (((1,), (0,)), ((), ())), preferred_element_type=F32)


def dot_nt(a, b):
    return lax.dot_general(a, b, (((1,), (1,)), ((), ())), preferred_element_type=F32)


def transposed(x):
    return jnp.transpose(x.astype(F32)).astype(BF)


def kernel(
    sizes,
    q_in, k_in, v_in, g_in, q_gain, k_gain,
    gq_out, gk_out, gv_out, gq_gain_out, gk_gain_out,
    q_buf, g_buf, k_buf, v_buf,
    q_unit, q_inv, k_unit, k_inv, stage,
    q_ext, q_low, q_unit_t, g_t, g_ext,
    k_raw, kv, v_t, k_t, e_s, ds_s, av_s, dq_t,
    dk_s, dv_s, dq_s,
    send_b, recv_b, send_r, recv_r,
    red_src, red_y, red_zx,
    in_sem, up_sem, down_sem,
    f_send, f_recv, s_send, s_recv, b_send, b_recv, r_send, r_recv,
    ys_sem, yr_sem, zs_sem, zr_sem,
):
    n_seq, n_head = sizes
    n_z = n_seq // (CORES * Y_LO)
    n_x = n_head // Y_HI
    n_y = Y_HI * Y_LO * CORES
    seq = lax.axis_index("seq")
    head = lax.axis_index("head")
    core = lax.rem(seq, CORES)
    y_lo = lax.rem(lax.div(seq, CORES), Y_LO)
    z = lax.div(seq, CORES * Y_LO)
    x = lax.rem(head, n_x)
    y_hi = lax.div(head, n_x)
    y_rank = (y_hi * Y_LO + y_lo) * CORES + core
    ahead = (seq + 2, head)
    behind = (seq - 2, head)
    sibling = (seq + 1 - 2 * core, head)
    z_step = CORES * Y_LO
    above = (seq + z_step, head)
    below = (seq - z_step, head)
    is_odd = core == 1
    is_even = core == 0
    has_ahead = seq < n_seq - 2
    has_behind = seq >= 2
    has_above = z < n_z - 1
    has_below = z > 0

    def y_peer(d):
        r = lax.rem(y_rank + d, n_y)
        c = lax.rem(r, CORES)
        yl = lax.rem(lax.div(r, CORES), Y_LO)
        yh = lax.div(r, CORES * Y_LO)
        return ((z * Y_LO + yl) * CORES + c, yh * n_x + x)

    def zx_peer(d):
        r = lax.rem(z * n_x + x + d, n_z * n_x)
        return ((lax.div(r, n_x) * Y_LO + y_lo) * CORES + core, y_hi * n_x + lax.rem(r, n_x))

    def x_peer(d):
        return (seq, y_hi * n_x + lax.rem(x + d, n_x))

    def signal(sem, dev):
        pl.semaphore_signal(sem, inc=1, device_id=dev, device_id_type=MESH)

    def remote(src, dst, ssem, rsem, dev):
        return pltpu.make_async_remote_copy(
            src_ref=src, dst_ref=dst, send_sem=ssem, recv_sem=rsem, device_id=dev, device_id_type=MESH
        )

    ins = [
        pltpu.make_async_copy(src, dst, in_sem.at[i])
        for i, (src, dst) in enumerate(
            ((k_in, k_buf), (v_in, v_buf), (q_in, q_buf), (g_in, g_buf))
        )
    ]
    for c in ins:
        c.start()

    barrier = pltpu.get_barrier_semaphore()
    always = [y_peer(d) for d in range(1, n_y)] + [x_peer(d) for d in range(1, n_x)]
    for p in always:
        signal(barrier, p)
    sometimes = ((has_ahead, ahead), (has_behind, behind), (has_above, above), (has_below, below))
    expected = jnp.int32(len(always))
    for there, p in sometimes:
        expected = expected + there.astype(jnp.int32)

        @pl.when(there)
        def _(p=p):
            signal(barrier, p)

    ok = [has_behind.astype(F32), (seq >= 1).astype(F32), jnp.float32(1.0)]

    @pl.when(jnp.logical_not(has_behind))
    def _():
        k_raw[0] = jnp.zeros((2 * T, D), BF)
        kv[0] = jnp.zeros((2, 2, T, D), BF)

    @pl.when(seq == 0)
    def _():
        k_raw[1] = jnp.zeros((2 * T, D), BF)
        kv[1] = jnp.zeros((2, 2, T, D), BF)

    @pl.when(jnp.logical_not(has_ahead))
    def _():
        recv_r[...] = jnp.zeros((2, 2, T, D), BF)

    def normalise(buf, unit, inv, rows):
        for r in range(0, rows, B):
            f = buf[r : r + B, :].astype(F32)
            i = lax.rsqrt(jnp.mean(f * f, axis=1, keepdims=True) + EPS)
            unit[r : r + B, :] = f * i
            inv[r : r + B, :] = jnp.broadcast_to(i, (B, D))

    kg = k_gain[...]
    qg = q_gain[...]
    def pieces(sh, own):
        return [k_in if own else k_raw.at[sh]] + [kv.at[2 if own else sh, kh, 1] for kh in range(2)]

    def hop(own, sh, ssem, rsem, dev):
        return [
            remote(src, dst, ssem.at[i], rsem.at[i], dev)
            for i, (src, dst) in enumerate(zip(pieces(0, own), pieces(sh, False)))
        ]

    fwd = hop(True, 0, f_send, f_recv, ahead)
    sib_own = hop(True, 1, s_send, s_recv, sibling)
    sib_fwd = hop(False, 1, s_send, s_recv, sibling)
    ret_b = [remote(send_b.at[kh], recv_b.at[kh], b_send.at[kh], b_recv.at[kh], sibling) for kh in range(2)]
    ret_r = [remote(send_r.at[kh], recv_r.at[kh], r_send.at[kh], r_recv.at[kh], behind) for kh in range(2)]

    def give(i):
        @pl.when(has_ahead)
        def _():
            fwd[i].start()

        @pl.when(is_even)
        def _():
            sib_own[i].start()

    pl.semaphore_wait(barrier, expected)
    give(0)
    ins[1].wait()
    stage[: 2 * T, :] = v_buf[...].astype(F32)
    for kh in range(2):
        kv[2, kh, 1] = stage[pl.ds(kh, T, stride=2), :].astype(BF)
    give(1)
    give(2)

    @pl.when(jnp.logical_not(has_below))
    def _():
        signal(up_sem, above)

    @pl.when(jnp.logical_not(has_above))
    def _():
        signal(down_sem, below)

    def pass_up():
        @pl.when(has_below)
        def _():
            pl.semaphore_wait(up_sem, 1)

            @pl.when(has_above)
            def _():
                signal(up_sem, above)

    def pass_down(low, high):
        @pl.when(has_above & (z >= low) & (z < high))
        def _():
            pl.semaphore_wait(down_sem, 1)

            @pl.when(has_below)
            def _():
                signal(down_sem, below)

    def rows_of(kh, qb, h):
        return pl.ds(4 * B * qb + 2 * kh + h, B, stride=4)

    ins[0].wait()
    normalise(k_buf, k_unit, k_inv, 2 * T)
    for kh in range(2):
        kv[2, kh, 0] = (k_unit[pl.ds(kh, T, stride=2), :] * kg).astype(BF)
    ins[2].wait()
    normalise(q_buf, q_unit, q_inv, 4 * T)
    ins[3].wait()
    stage[...] = g_buf[...].astype(F32)
    for kh in range(2):
        for qb in range(2):
            for h in range(2):
                rows = rows_of(kh, qb, h)
                unit = q_unit[rows, :]
                low = (unit * qg).astype(BF)
                scaled = low.astype(F32) * EXP2_SCALE
                high = scaled.astype(BF)
                rest = (scaled - high.astype(F32)).astype(BF)
                at = slice(h * B, (h + 1) * B)
                q_low[kh, qb, at, :] = low
                q_unit_t[kh, qb, :, at] = jnp.transpose(unit)
                q_ext[kh, qb, at, :D] = high
                q_ext[kh, qb, at, D:] = rest
                g_t[kh, qb, :, at] = jnp.transpose(stage[rows, :]).astype(BF)

    def prepare_k(sh):
        if sh < 2:
            for r in range(0, 2 * T, B):
                f = k_raw[sh, r : r + B, :].astype(F32)
                i = lax.rsqrt(jnp.mean(f * f, axis=1, keepdims=True) + EPS)
                stage[r : r + B, :] = f * i * kg
        for kh in range(2):
            if sh < 2:
                kv[sh, kh, 0] = stage[pl.ds(kh, T, stride=2), :].astype(BF)
            k_t[kh, :, sh * T : (sh + 1) * T] = transposed(kv[sh, kh, 0])

    def prepare_v(sh, kh):
        span = slice(sh * T, (sh + 1) * T)
        v_t[kh, :D, span] = transposed(kv[sh, kh, 1])
        v_t[kh, D:, span] = jnp.full((EXT, T), ok[sh], F32).astype(BF)

    key_row = lax.broadcasted_iota(jnp.int32, (B, 2 * B), 0)
    query_col = lax.rem(lax.broadcasted_iota(jnp.int32, (B, 2 * B), 1), B)

    def weigh(kh, qb, r0, r1):
        off = qb * B
        for b in range(r0, r1, B):
            k = kv[b // T, kh, 0, b % T : b % T + B, :]
            s = dot_nt(jnp.concatenate([k, k], axis=1), q_ext[kh, qb])
            e = jnp.exp2(s)
            if b == off:
                e = jnp.where(key_row > query_col, e, 0.0)
            if b == off + WINDOW:
                e = jnp.where(key_row <= query_col, e, 0.0)
            e_s[kh, qb, b - off : b - off + B, :] = e.astype(BF)

    def attend(kh, qb, r0, r1, first):
        off = qb * B
        av = dot_nn(v_t[kh, :, r0:r1], e_s[kh, qb, r0 - off : r1 - off, :])
        if first:
            av_s[kh, qb] = av
        else:
            av_s[kh, qb] += av

    def finish(kh, qb):
        l_row = av_s[kh, qb, D : D + 1, :]
        inv = 1.0 / l_row
        scaled = (g_t[kh, qb].astype(F32) * inv).astype(BF)
        g_ext[kh, qb, :D, :] = scaled
        off = -inv * jnp.sum(scaled.astype(F32) * av_s[kh, qb, :D, :], axis=0, keepdims=True)
        high = off.astype(BF).astype(F32)
        rest = off - high
        row = lax.broadcasted_iota(jnp.int32, (EXT, 2 * B), 0)
        tail = jnp.where(row == 0, high, jnp.where(row == 1, rest, 0.0))
        g_ext[kh, qb, D : D + EXT, :] = tail.astype(BF)
        g_ext[kh, qb, D + EXT :, :] = jnp.zeros((D - EXT, 2 * B), BF)

    def score_grads(kh, qb, r0, r1):
        off = qb * B
        for b in range(r0, r1, B):
            sh = b // T
            ones = jnp.full((B, D), ok[sh], F32).astype(BF)
            vx = jnp.concatenate([kv[sh, kh, 1, b % T : b % T + B, :], ones], axis=1)
            dp = dot_nn(vx, g_ext[kh, qb])
            e = e_s[kh, qb, b - off : b - off + B, :]
            ds_s[qb, b - off : b - off + B, :] = e * dp.astype(BF)

    def query_grads(kh, qb):
        off = qb * B
        dq_t[kh, qb] = dot_nn(k_t[kh, :, off : off + WINDOW + B], ds_s[qb])

    def key_grads(kh, qb, r0, r1, first_of):
        off = qb * B
        for b in range(r0, r1, B):
            at = slice(b - off, b - off + B)
            dv = dot_nt(e_s[kh, qb, at, :], g_ext[kh, qb, :D, :])
            dk = dot_nn(ds_s[qb, at, :], q_low[kh, qb])
            if first_of(b):
                dv_s[kh, b : b + B, :] = dv
                dk_s[kh, b : b + B, :] = dk
            else:
                dv_s[kh, b : b + B, :] += dv
                dk_s[kh, b : b + B, :] += dk

    prepare_k(2)
    for kh in range(2):
        weigh(kh, 0, 2 * T, 2 * T + B)
        weigh(kh, 1, 2 * T, 3 * T)
    for kh in range(2):
        prepare_v(2, kh)
        attend(kh, 0, 2 * T, 2 * T + B, True)
        attend(kh, 1, 2 * T, 3 * T, True)

    odd_f = is_odd.astype(F32)
    even_f = is_even.astype(F32)

    def take(p):
        @pl.when(has_behind)
        def _():
            fwd[p].wait_recv()

            @pl.when(is_odd)
            def _():
                sib_fwd[p].start()

    def take_b(p):
        @pl.when(seq >= 1)
        def _():
            sib_own[p].wait_recv()

    def pay_back(kh):
        ret_b[kh].wait_recv()
        send_r[kh, 0] = (dk_s[kh, :T, :] * SCALE + recv_b[kh, 0].astype(F32) * odd_f).astype(BF)
        send_r[kh, 1] = (dv_s[kh, :T, :] + recv_b[kh, 1].astype(F32) * odd_f).astype(BF)

        @pl.when(has_behind)
        def _():
            ret_r[kh].start()

    pass_up()
    pass_down(n_z - 3, n_z)
    take(0)
    prepare_k(0)
    take_b(0)
    prepare_k(1)
    for kh in range(2):
        weigh(kh, 0, 0, 2 * T)
        weigh(kh, 1, B, 2 * T)

    def remote_key_grads(kh):
        key_grads(kh, 0, 0, 2 * T, lambda b: True)
        key_grads(kh, 1, B, 2 * T, lambda b: b >= 2 * T)
        send_b[kh, 0] = (dk_s[kh, T : 2 * T, :] * SCALE).astype(BF)
        send_b[kh, 1] = dv_s[kh, T : 2 * T, :].astype(BF)
        ret_b[kh].start()

    def own_key_grads(kh):
        key_grads(kh, 0, 2 * T, 2 * T + B, lambda b: True)
        key_grads(kh, 1, 2 * T, 3 * T, lambda b: b >= 2 * T + B)

    def lay_out_queries(kh):
        for qb in range(2):
            for h in range(2):
                dq_s[rows_of(kh, qb, h), :] = jnp.transpose(dq_t[kh, qb, :, h * B : (h + 1) * B]) * SCALE

    gain_sum = jnp.zeros((D, D), F32)
    for kh in range(2):
        if kh == 0:
            take(1)
        prepare_v(0, kh)
        take_b(1 + kh)
        prepare_v(1, kh)
        attend(kh, 0, 0, 2 * T, False)
        attend(kh, 1, B, 2 * T, False)
        finish(kh, 0)
        finish(kh, 1)
        for qb in range(2):
            score_grads(kh, qb, qb * B, qb * B + WINDOW + B)
            query_grads(kh, qb)
            prod = dq_t[kh, qb] * q_unit_t[kh, qb]
            for c in range(0, 2 * B, D):
                gain_sum = gain_sum + prod[:, c : c + D]
        if kh == 0:
            remote_key_grads(0)
            take(2)
            own_key_grads(0)
            pay_back(0)
            pass_down(n_z - 5, n_z - 3)
    pass_down(0, n_z - 5)

    q_row = jnp.sum(jnp.transpose(gain_sum), axis=0, keepdims=True) * SCALE
    red_src[0] = q_row

    def exchange(level, dst, ssem, rsem, peer, count):
        copies = [
            remote(red_src.at[level], dst.at[d - 1], ssem.at[d - 1], rsem.at[d - 1], peer(d))
            for d in range(1, count)
        ]
        for c in copies:
            c.start()
        return copies

    def absorb(level, dst, copies):
        for c in copies:
            c.wait_recv()
        total = red_src[level]
        for d in range(len(copies)):
            total = total + dst[d]
        red_src[level + 1] = total

    def norm_back(grad, unit, inv, gain, out, rows):
        for r in range(0, rows, B):
            u = unit[r : r + B, :]
            du = grad[r : r + B, :] * gain
            m = jnp.mean(du * u, axis=1, keepdims=True)
            out[r : r + B, :] = (inv[r : r + B, :] * (du - u * m)).astype(BF)

    zx_copies = exchange(0, red_zx, zs_sem, zr_sem, zx_peer, n_z * n_x)
    remote_key_grads(1)
    own_key_grads(1)
    pay_back(1)
    lay_out_queries(0)
    lay_out_queries(1)
    norm_back(dq_s, q_unit, q_inv, qg, gq_out, 4 * T)
    absorb(0, red_zx, zx_copies)
    y_copies = exchange(1, red_y, ys_sem, yr_sem, y_peer, n_y)

    for kh in range(2):

        @pl.when(has_ahead)
        def _(kh=kh):
            ret_r[kh].wait_recv()

        rows = pl.ds(kh, T, stride=2)
        dq_s[rows, :] = (
            dk_s[kh, 2 * T :, :] * SCALE
            + recv_r[kh, 0].astype(F32)
            + recv_b[kh, 0].astype(F32) * even_f
        )
        stage[rows, :] = (
            dv_s[kh, 2 * T :, :] + recv_r[kh, 1].astype(F32) + recv_b[kh, 1].astype(F32) * even_f
        )
    norm_back(dq_s, k_unit, k_inv, kg, gk_out, 2 * T)
    gv_out[...] = stage[: 2 * T, :].astype(BF)
    absorb(1, red_y, y_copies)
    gq_gain_out[...] = red_src[2]
    gk_gain_out[...] = red_src[2] * qg / kg

    for c in y_copies + zx_copies + ret_b:
        c.wait_send()

    @pl.when(has_ahead)
    def _():
        for c in fwd:
            c.wait_send()

    @pl.when(is_even | has_behind)
    def _():
        for c in sib_own:
            c.wait_send()

    @pl.when(has_behind)
    def _():
        for kh in range(2):
            ret_r[kh].wait_send()


def write_out(*refs):
    sem = refs[-1]
    n = (len(refs) - 1) // 2
    copies = [pltpu.make_async_copy(refs[i], refs[n + i], sem.at[i]) for i in range(n)]
    for c in copies:
        c.start()
    for c in copies:
        c.wait()


def per_device(n_seq, n_head, query, key, value, grad_out, q_gain, k_gain):
    n_y = Y_HI * Y_LO * CORES
    n_z = n_seq // (CORES * Y_LO)
    n_x = n_head // Y_HI
    hbm = pl.BlockSpec(memory_space=pl.ANY)
    vmem = pl.BlockSpec(memory_space=pltpu.VMEM)
    dma = pltpu.SemaphoreType.DMA
    scratch = [
        pltpu.VMEM((4 * T, D), BF), pltpu.VMEM((4 * T, D), BF),
        pltpu.VMEM((2 * T, D), BF), pltpu.VMEM((2 * T, D), BF),
        pltpu.VMEM((4 * T, D), F32), pltpu.VMEM((4 * T, D), F32),
        pltpu.VMEM((2 * T, D), F32), pltpu.VMEM((2 * T, D), F32),
        pltpu.VMEM((4 * T, D), F32),
        pltpu.VMEM((2, 2, 2 * B, 2 * D), BF), pltpu.VMEM((2, 2, 2 * B, D), BF),
        pltpu.VMEM((2, 2, D, 2 * B), F32),
        pltpu.VMEM((2, 2, D, 2 * B), BF), pltpu.VMEM((2, 2, 2 * D, 2 * B), BF),
        pltpu.VMEM((2, 2 * T, D), BF),
        pltpu.VMEM((3, 2, 2, T, D), BF),
        pltpu.VMEM((2, D + EXT, KEYS), BF),
        pltpu.VMEM((2, D, KEYS), BF),
        pltpu.VMEM((2, 2, WINDOW + B, 2 * B), BF),
        pltpu.VMEM((2, WINDOW + B, 2 * B), BF),
        pltpu.VMEM((2, 2, D + EXT, 2 * B), F32),
        pltpu.VMEM((2, 2, D, 2 * B), F32),
        pltpu.VMEM((2, KEYS, D), F32), pltpu.VMEM((2, KEYS, D), F32),
        pltpu.VMEM((4 * T, D), F32),
        pltpu.VMEM((2, 2, T, D), BF), pltpu.VMEM((2, 2, T, D), BF),
        pltpu.VMEM((2, 2, T, D), BF), pltpu.VMEM((2, 2, T, D), BF),
        pltpu.VMEM((3, 1, D), F32),
        pltpu.VMEM((n_y - 1, 1, D), F32),
        pltpu.VMEM((n_z * n_x - 1, 1, D), F32),
        dma((4,)), pltpu.SemaphoreType.REGULAR, pltpu.SemaphoreType.REGULAR,
        dma((3,)), dma((3,)), dma((3,)), dma((3,)), dma((2,)), dma((2,)), dma((2,)), dma((2,)),
        dma((n_y - 1,)), dma((n_y - 1,)),
        dma((n_z * n_x - 1,)), dma((n_z * n_x - 1,)),
    ]
    shapes = [((4 * T, D), BF), ((2 * T, D), BF), ((2 * T, D), BF), ((1, D), F32), ((1, D), F32)]
    held = pl.pallas_call(
        functools.partial(kernel, (n_seq, n_head)),
        out_shape=[pltpu.VMEM(*s) for s in shapes],
        in_specs=[hbm] * 4 + [vmem] * 2,
        out_specs=[vmem] * len(shapes),
        scratch_shapes=scratch,
        compiler_params=pltpu.CompilerParams(collective_id=0, has_side_effects=True),
        name="swa_backward",
    )(
        query.reshape(4 * T, D),
        key.reshape(2 * T, D),
        value.reshape(2 * T, D),
        grad_out.reshape(4 * T, D),
        q_gain.reshape(1, D),
        k_gain.reshape(1, D),
    )
    gq, gk, gv, gq_gain, gk_gain = pl.pallas_call(
        write_out,
        out_shape=[jax.ShapeDtypeStruct(*s) for s in shapes],
        in_specs=[vmem] * len(shapes),
        out_specs=[hbm] * len(shapes),
        scratch_shapes=[dma((len(shapes),))],
        name="write_out",
    )(*[pltpu.with_memory_space_constraint(a, pltpu.VMEM) for a in held])
    return (
        gq.reshape(T, 4, D),
        gk.reshape(T, 2, D),
        gv.reshape(T, 2, D),
        gq_gain.reshape(D),
        gk_gain.reshape(D),
    )


def solution(mesh):
    split = P("seq", "head", None)
    return jax.shard_map(
        functools.partial(per_device, mesh.shape["seq"], mesh.shape["head"]),
        mesh=mesh,
        in_specs=(split, split, split, split, P(), P()),
        out_specs=(split, split, split, P(), P()),
        check_vma=False,
    )
```

```python
import functools
import math

import jax
import jax.numpy as jnp
from jax import lax
from jax.experimental import pallas as pl
from jax.experimental.pallas import tpu as pltpu
from jax.sharding import PartitionSpec as P

WINDOW = 1024
SCALE = 168.0 ** (-0.5)
EXP2_SCALE = SCALE * math.log2(math.e)
EPS = 1e-06
CORES = 2
Y_LO = 4
Y_HI = 2

BF = jnp.bfloat16
F32 = jnp.float32
MESH = pl.DeviceIdType.MESH

T = 512
D = 128
B = 256
KEYS = 3 * T
EXT = 16


def dot_nn(a, b):
    return lax.dot_general(a, b, (((1,), (0,)), ((), ())), preferred_element_type=F32)


def dot_nt(a, b):
    return lax.dot_general(a, b, (((1,), (1,)), ((), ())), preferred_element_type=F32)


def transposed(x):
    return jnp.transpose(x.astype(F32)).astype(BF)


def kernel(
    sizes,
    q_in, k_in, v_in, g_in, q_gain_in, k_gain_in,
    gq_out, gk_out, gv_out, gq_gain_out, gk_gain_out,
    q_buf, g_buf, k_buf, v_buf,
    q_unit, q_inv, k_unit, k_inv, stage,
    q_ext, q_low, q_unit_t, g_t, g_ext,
    k_raw, kv, v_t, k_t, e_s, ds_s, av_s, dq_t,
    dk_s, dv_s, dq_s,
    send_b, recv_b, send_r, recv_r,
    red_src, red_y, red_zx,
    gains, in_sem, up_sem, down_sem,
    f_send, f_recv, s_send, s_recv, b_send, b_recv, r_send, r_recv,
    ys_sem, yr_sem, zs_sem, zr_sem,
):
    n_seq, n_head = sizes
    n_z = n_seq // (CORES * Y_LO)
    n_x = n_head // Y_HI
    n_y = Y_HI * Y_LO * CORES
    seq = lax.axis_index("seq")
    head = lax.axis_index("head")
    core = lax.rem(seq, CORES)
    y_lo = lax.rem(lax.div(seq, CORES), Y_LO)
    z = lax.div(seq, CORES * Y_LO)
    x = lax.rem(head, n_x)
    y_hi = lax.div(head, n_x)
    y_rank = (y_hi * Y_LO + y_lo) * CORES + core
    ahead = (seq + 2, head)
    behind = (seq - 2, head)
    sibling = (seq + 1 - 2 * core, head)
    z_step = CORES * Y_LO
    above = (seq + z_step, head)
    below = (seq - z_step, head)
    is_odd = core == 1
    is_even = core == 0
    has_ahead = seq < n_seq - 2
    has_behind = seq >= 2
    has_above = z < n_z - 1
    has_below = z > 0

    def y_peer(d):
        r = lax.rem(y_rank + d, n_y)
        c = lax.rem(r, CORES)
        yl = lax.rem(lax.div(r, CORES), Y_LO)
        yh = lax.div(r, CORES * Y_LO)
        return ((z * Y_LO + yl) * CORES + c, yh * n_x + x)

    def zx_peer(d):
        r = lax.rem(z * n_x + x + d, n_z * n_x)
        return ((lax.div(r, n_x) * Y_LO + y_lo) * CORES + core, y_hi * n_x + lax.rem(r, n_x))

    def x_peer(d):
        return (seq, y_hi * n_x + lax.rem(x + d, n_x))

    def signal(sem, dev):
        pl.semaphore_signal(sem, inc=1, device_id=dev, device_id_type=MESH)

    def remote(src, dst, ssem, rsem, dev):
        return pltpu.make_async_remote_copy(
            src_ref=src, dst_ref=dst, send_sem=ssem, recv_sem=rsem, device_id=dev, device_id_type=MESH
        )

    ins = [
        pltpu.make_async_copy(src, dst, in_sem.at[i])
        for i, (src, dst) in enumerate(
            (
                (k_in, k_buf), (v_in, v_buf), (q_in, q_buf), (g_in, g_buf),
                (q_gain_in, gains.at[0]), (k_gain_in, gains.at[1]),
            )
        )
    ]
    for c in ins:
        c.start()

    barrier = pltpu.get_barrier_semaphore()
    always = [y_peer(d) for d in range(1, n_y)] + [x_peer(d) for d in range(1, n_x)]
    for p in always:
        signal(barrier, p)
    sometimes = ((has_ahead, ahead), (has_behind, behind), (has_above, above), (has_below, below))
    expected = jnp.int32(len(always))
    for there, p in sometimes:
        expected = expected + there.astype(jnp.int32)

        @pl.when(there)
        def _(p=p):
            signal(barrier, p)

    ok = [has_behind.astype(F32), (seq >= 1).astype(F32), jnp.float32(1.0)]

    @pl.when(jnp.logical_not(has_behind))
    def _():
        k_raw[0] = jnp.zeros((2 * T, D), BF)
        kv[0] = jnp.zeros((2, 2, T, D), BF)

    @pl.when(seq == 0)
    def _():
        k_raw[1] = jnp.zeros((2 * T, D), BF)
        kv[1] = jnp.zeros((2, 2, T, D), BF)

    @pl.when(jnp.logical_not(has_ahead))
    def _():
        recv_r[...] = jnp.zeros((2, 2, T, D), BF)

    def normalise(buf, unit, inv, rows):
        for r in range(0, rows, B):
            f = buf[r : r + B, :].astype(F32)
            i = lax.rsqrt(jnp.mean(f * f, axis=1, keepdims=True) + EPS)
            unit[r : r + B, :] = f * i
            inv[r : r + B, :] = jnp.broadcast_to(i, (B, D))

    def pieces(sh, own):
        return [k_in if own else k_raw.at[sh]] + [kv.at[2 if own else sh, kh, 1] for kh in range(2)]

    def hop(own, sh, ssem, rsem, dev):
        return [
            remote(src, dst, ssem.at[i], rsem.at[i], dev)
            for i, (src, dst) in enumerate(zip(pieces(0, own), pieces(sh, False)))
        ]

    fwd = hop(True, 0, f_send, f_recv, ahead)
    sib_own = hop(True, 1, s_send, s_recv, sibling)
    sib_fwd = hop(False, 1, s_send, s_recv, sibling)
    ret_b = [remote(send_b.at[kh], recv_b.at[kh], b_send.at[kh], b_recv.at[kh], sibling) for kh in range(2)]
    ret_r = [remote(send_r.at[kh], recv_r.at[kh], r_send.at[kh], r_recv.at[kh], behind) for kh in range(2)]

    def give(i):
        @pl.when(has_ahead)
        def _():
            fwd[i].start()

        @pl.when(is_even)
        def _():
            sib_own[i].start()

    pl.semaphore_wait(barrier, expected)
    give(0)
    ins[1].wait()
    stage[: 2 * T, :] = v_buf[...].astype(F32)
    for kh in range(2):
        kv[2, kh, 1] = stage[pl.ds(kh, T, stride=2), :].astype(BF)
    give(1)
    give(2)

    @pl.when(jnp.logical_not(has_below))
    def _():
        signal(up_sem, above)

    @pl.when(jnp.logical_not(has_above))
    def _():
        signal(down_sem, below)

    def pass_up():
        @pl.when(has_below)
        def _():
            pl.semaphore_wait(up_sem, 1)

            @pl.when(has_above)
            def _():
                signal(up_sem, above)

    def pass_down(low, high):
        @pl.when(has_above & (z >= low) & (z < high))
        def _():
            pl.semaphore_wait(down_sem, 1)

            @pl.when(has_below)
            def _():
                signal(down_sem, below)

    def rows_of(kh, qb, h):
        return pl.ds(4 * B * qb + 2 * kh + h, B, stride=4)

    ins[4].wait()
    ins[5].wait()
    qg = gains[0]
    kg = gains[1]
    ins[0].wait()
    normalise(k_buf, k_unit, k_inv, 2 * T)
    for kh in range(2):
        kv[2, kh, 0] = (k_unit[pl.ds(kh, T, stride=2), :] * kg).astype(BF)
    ins[2].wait()
    normalise(q_buf, q_unit, q_inv, 4 * T)
    ins[3].wait()
    stage[...] = g_buf[...].astype(F32)
    for kh in range(2):
        for qb in range(2):
            for h in range(2):
                rows = rows_of(kh, qb, h)
                unit = q_unit[rows, :]
                low = (unit * qg).astype(BF)
                scaled = low.astype(F32) * EXP2_SCALE
                high = scaled.astype(BF)
                rest = (scaled - high.astype(F32)).astype(BF)
                at = slice(h * B, (h + 1) * B)
                q_low[kh, qb, at, :] = low
                q_unit_t[kh, qb, :, at] = jnp.transpose(unit)
                q_ext[kh, qb, at, :D] = high
                q_ext[kh, qb, at, D:] = rest
                g_t[kh, qb, :, at] = jnp.transpose(stage[rows, :]).astype(BF)

    def prepare_k(sh):
        if sh < 2:
            for r in range(0, 2 * T, B):
                f = k_raw[sh, r : r + B, :].astype(F32)
                i = lax.rsqrt(jnp.mean(f * f, axis=1, keepdims=True) + EPS)
                stage[r : r + B, :] = f * i * kg
        for kh in range(2):
            if sh < 2:
                kv[sh, kh, 0] = stage[pl.ds(kh, T, stride=2), :].astype(BF)
            k_t[kh, :, sh * T : (sh + 1) * T] = transposed(kv[sh, kh, 0])

    def prepare_v(sh, kh):
        span = slice(sh * T, (sh + 1) * T)
        v_t[kh, :D, span] = transposed(kv[sh, kh, 1])
        v_t[kh, D:, span] = jnp.full((EXT, T), ok[sh], F32).astype(BF)

    key_row = lax.broadcasted_iota(jnp.int32, (B, 2 * B), 0)
    query_col = lax.rem(lax.broadcasted_iota(jnp.int32, (B, 2 * B), 1), B)

    def weigh(kh, qb, r0, r1):
        off = qb * B
        for b in range(r0, r1, B):
            k = kv[b // T, kh, 0, b % T : b % T + B, :]
            s = dot_nt(jnp.concatenate([k, k], axis=1), q_ext[kh, qb])
            e = jnp.exp2(s)
            if b == off:
                e = jnp.where(key_row > query_col, e, 0.0)
            if b == off + WINDOW:
                e = jnp.where(key_row <= query_col, e, 0.0)
            e_s[kh, qb, b - off : b - off + B, :] = e.astype(BF)

    def attend(kh, qb, r0, r1, first):
        off = qb * B
        av = dot_nn(v_t[kh, :, r0:r1], e_s[kh, qb, r0 - off : r1 - off, :])
        if first:
            av_s[kh, qb] = av
        else:
            av_s[kh, qb] += av

    def finish(kh, qb):
        l_row = av_s[kh, qb, D : D + 1, :]
        inv = 1.0 / l_row
        scaled = (g_t[kh, qb].astype(F32) * inv).astype(BF)
        g_ext[kh, qb, :D, :] = scaled
        off = -inv * jnp.sum(scaled.astype(F32) * av_s[kh, qb, :D, :], axis=0, keepdims=True)
        high = off.astype(BF).astype(F32)
        rest = off - high
        row = lax.broadcasted_iota(jnp.int32, (EXT, 2 * B), 0)
        tail = jnp.where(row == 0, high, jnp.where(row == 1, rest, 0.0))
        g_ext[kh, qb, D : D + EXT, :] = tail.astype(BF)
        g_ext[kh, qb, D + EXT :, :] = jnp.zeros((D - EXT, 2 * B), BF)

    def score_grads(kh, qb, r0, r1):
        off = qb * B
        for b in range(r0, r1, B):
            sh = b // T
            ones = jnp.full((B, D), ok[sh], F32).astype(BF)
            vx = jnp.concatenate([kv[sh, kh, 1, b % T : b % T + B, :], ones], axis=1)
            dp = dot_nn(vx, g_ext[kh, qb])
            e = e_s[kh, qb, b - off : b - off + B, :]
            ds_s[kh, qb, b - off : b - off + B, :] = e * dp.astype(BF)

    def query_grads(kh, qb):
        off = qb * B
        dq_t[kh, qb] = dot_nn(k_t[kh, :, off : off + WINDOW + B], ds_s[kh, qb])

    def key_grads(kh, qb, r0, r1, first_of):
        off = qb * B
        for b in range(r0, r1, B):
            at = slice(b - off, b - off + B)
            dv = dot_nt(e_s[kh, qb, at, :], g_ext[kh, qb, :D, :])
            dk = dot_nn(ds_s[kh, qb, at, :], q_low[kh, qb])
            if first_of(b):
                dv_s[kh, b : b + B, :] = dv
                dk_s[kh, b : b + B, :] = dk
            else:
                dv_s[kh, b : b + B, :] += dv
                dk_s[kh, b : b + B, :] += dk

    prepare_k(2)
    for kh in range(2):
        weigh(kh, 0, 2 * T, 2 * T + B)
        weigh(kh, 1, 2 * T, 3 * T)
    for kh in range(2):
        prepare_v(2, kh)
        attend(kh, 0, 2 * T, 2 * T + B, True)
        attend(kh, 1, 2 * T, 3 * T, True)

    odd_f = is_odd.astype(F32)
    even_f = is_even.astype(F32)

    def take(p):
        @pl.when(has_behind)
        def _():
            fwd[p].wait_recv()

            @pl.when(is_odd)
            def _():
                sib_fwd[p].start()

    def take_b(p):
        @pl.when(seq >= 1)
        def _():
            sib_own[p].wait_recv()

    def pay_back(kh):
        ret_b[kh].wait_recv()
        send_r[kh, 0] = (dk_s[kh, :T, :] * SCALE + recv_b[kh, 0].astype(F32) * odd_f).astype(BF)
        send_r[kh, 1] = (dv_s[kh, :T, :] + recv_b[kh, 1].astype(F32) * odd_f).astype(BF)

        @pl.when(has_behind)
        def _():
            ret_r[kh].start()

    pass_up()
    pass_down(n_z - 3, n_z)
    take(0)
    prepare_k(0)
    take_b(0)
    prepare_k(1)
    for kh in range(2):
        weigh(kh, 0, 0, 2 * T)
        weigh(kh, 1, B, 2 * T)

    def remote_key_grads(kh):
        key_grads(kh, 0, 0, 2 * T, lambda b: True)
        key_grads(kh, 1, B, 2 * T, lambda b: b >= 2 * T)
        send_b[kh, 0] = (dk_s[kh, T : 2 * T, :] * SCALE).astype(BF)
        send_b[kh, 1] = dv_s[kh, T : 2 * T, :].astype(BF)
        ret_b[kh].start()

    def own_key_grads(kh):
        key_grads(kh, 0, 2 * T, 2 * T + B, lambda b: True)
        key_grads(kh, 1, 2 * T, 3 * T, lambda b: b >= 2 * T + B)

    def lay_out_queries(kh):
        for qb in range(2):
            for h in range(2):
                dq_s[rows_of(kh, qb, h), :] = jnp.transpose(dq_t[kh, qb, :, h * B : (h + 1) * B]) * SCALE

    gain_sum = jnp.zeros((D, D), F32)
    for kh in range(2):
        if kh == 0:
            take(1)
        prepare_v(0, kh)
        take_b(1 + kh)
        prepare_v(1, kh)
        attend(kh, 0, 0, 2 * T, False)
        attend(kh, 1, B, 2 * T, False)
        finish(kh, 0)
        finish(kh, 1)
        for qb in range(2):
            score_grads(kh, qb, qb * B, qb * B + WINDOW + B)
            query_grads(kh, qb)
            prod = dq_t[kh, qb] * q_unit_t[kh, qb]
            for c in range(0, 2 * B, D):
                gain_sum = gain_sum + prod[:, c : c + D]
        if kh == 0:
            remote_key_grads(0)
            take(2)
            pay_back(0)
            pass_down(n_z - 4, n_z - 3)
    pass_down(0, n_z - 4)

    q_row = jnp.sum(jnp.transpose(gain_sum), axis=0, keepdims=True) * SCALE
    red_src[0] = q_row

    def exchange(level, dst, ssem, rsem, peer, count):
        copies = [
            remote(red_src.at[level], dst.at[d - 1], ssem.at[d - 1], rsem.at[d - 1], peer(d))
            for d in range(1, count)
        ]
        for c in copies:
            c.start()
        return copies

    def absorb(level, dst, copies):
        for c in copies:
            c.wait_recv()
        total = red_src[level]
        for d in range(len(copies)):
            total = total + dst[d]
        red_src[level + 1] = total

    def norm_back(grad, unit, inv, gain, out, rows):
        for r in range(0, rows, B):
            u = unit[r : r + B, :]
            du = grad[r : r + B, :] * gain
            m = jnp.mean(du * u, axis=1, keepdims=True)
            out[r : r + B, :] = (inv[r : r + B, :] * (du - u * m)).astype(BF)

    zx_copies = exchange(0, red_zx, zs_sem, zr_sem, zx_peer, n_z * n_x)
    remote_key_grads(1)
    own_key_grads(0)
    pay_back(1)
    own_key_grads(1)
    lay_out_queries(0)
    lay_out_queries(1)
    norm_back(dq_s, q_unit, q_inv, qg, gq_out, 4 * T)
    absorb(0, red_zx, zx_copies)
    y_copies = exchange(1, red_y, ys_sem, yr_sem, y_peer, n_y)

    for kh in range(2):

        @pl.when(has_ahead)
        def _(kh=kh):
            ret_r[kh].wait_recv()

        rows = pl.ds(kh, T, stride=2)
        dq_s[rows, :] = (
            dk_s[kh, 2 * T :, :] * SCALE
            + recv_r[kh, 0].astype(F32)
            + recv_b[kh, 0].astype(F32) * even_f
        )
        stage[rows, :] = (
            dv_s[kh, 2 * T :, :] + recv_r[kh, 1].astype(F32) + recv_b[kh, 1].astype(F32) * even_f
        )
    norm_back(dq_s, k_unit, k_inv, kg, gk_out, 2 * T)
    gv_out[...] = stage[: 2 * T, :].astype(BF)
    absorb(1, red_y, y_copies)
    gq_gain_out[...] = red_src[2]
    gk_gain_out[...] = red_src[2] * qg / kg

    for c in y_copies + zx_copies + ret_b:
        c.wait_send()

    @pl.when(has_ahead)
    def _():
        for c in fwd:
            c.wait_send()

    @pl.when(is_even | has_behind)
    def _():
        for c in sib_own:
            c.wait_send()

    @pl.when(has_behind)
    def _():
        for kh in range(2):
            ret_r[kh].wait_send()


def write_out(*refs):
    sem = refs[-1]
    n = (len(refs) - 1) // 2
    copies = [pltpu.make_async_copy(refs[i], refs[n + i], sem.at[i]) for i in range(n)]
    for c in copies:
        c.start()
    for c in copies:
        c.wait()


def per_device(n_seq, n_head, query, key, value, grad_out, q_gain, k_gain):
    n_y = Y_HI * Y_LO * CORES
    n_z = n_seq // (CORES * Y_LO)
    n_x = n_head // Y_HI
    hbm = pl.BlockSpec(memory_space=pl.ANY)
    vmem = pl.BlockSpec(memory_space=pltpu.VMEM)
    dma = pltpu.SemaphoreType.DMA
    scratch = [
        pltpu.VMEM((4 * T, D), BF), pltpu.VMEM((4 * T, D), BF),
        pltpu.VMEM((2 * T, D), BF), pltpu.VMEM((2 * T, D), BF),
        pltpu.VMEM((4 * T, D), F32), pltpu.VMEM((4 * T, D), F32),
        pltpu.VMEM((2 * T, D), F32), pltpu.VMEM((2 * T, D), F32),
        pltpu.VMEM((4 * T, D), F32),
        pltpu.VMEM((2, 2, 2 * B, 2 * D), BF), pltpu.VMEM((2, 2, 2 * B, D), BF),
        pltpu.VMEM((2, 2, D, 2 * B), F32),
        pltpu.VMEM((2, 2, D, 2 * B), BF), pltpu.VMEM((2, 2, 2 * D, 2 * B), BF),
        pltpu.VMEM((2, 2 * T, D), BF),
        pltpu.VMEM((3, 2, 2, T, D), BF),
        pltpu.VMEM((2, D + EXT, KEYS), BF),
        pltpu.VMEM((2, D, KEYS), BF),
        pltpu.VMEM((2, 2, WINDOW + B, 2 * B), BF),
        pltpu.VMEM((2, 2, WINDOW + B, 2 * B), BF),
        pltpu.VMEM((2, 2, D + EXT, 2 * B), F32),
        pltpu.VMEM((2, 2, D, 2 * B), F32),
        pltpu.VMEM((2, KEYS, D), F32), pltpu.VMEM((2, KEYS, D), F32),
        pltpu.VMEM((4 * T, D), F32),
        pltpu.VMEM((2, 2, T, D), BF), pltpu.VMEM((2, 2, T, D), BF),
        pltpu.VMEM((2, 2, T, D), BF), pltpu.VMEM((2, 2, T, D), BF),
        pltpu.VMEM((3, 1, D), F32),
        pltpu.VMEM((n_y - 1, 1, D), F32),
        pltpu.VMEM((n_z * n_x - 1, 1, D), F32),
        pltpu.VMEM((2, 1, D), F32),
        dma((6,)), pltpu.SemaphoreType.REGULAR, pltpu.SemaphoreType.REGULAR,
        dma((3,)), dma((3,)), dma((3,)), dma((3,)), dma((2,)), dma((2,)), dma((2,)), dma((2,)),
        dma((n_y - 1,)), dma((n_y - 1,)),
        dma((n_z * n_x - 1,)), dma((n_z * n_x - 1,)),
    ]
    shapes = [((4 * T, D), BF), ((2 * T, D), BF), ((2 * T, D), BF), ((1, D), F32), ((1, D), F32)]
    held = pl.pallas_call(
        functools.partial(kernel, (n_seq, n_head)),
        out_shape=[pltpu.VMEM(*s) for s in shapes],
        in_specs=[hbm] * 6,
        out_specs=[vmem] * len(shapes),
        scratch_shapes=scratch,
        compiler_params=pltpu.CompilerParams(collective_id=0, has_side_effects=True),
        name="swa_backward",
    )(
        query.reshape(4 * T, D),
        key.reshape(2 * T, D),
        value.reshape(2 * T, D),
        grad_out.reshape(4 * T, D),
        q_gain.reshape(1, D),
        k_gain.reshape(1, D),
    )
    gq, gk, gv, gq_gain, gk_gain = pl.pallas_call(
        write_out,
        out_shape=[jax.ShapeDtypeStruct(*s) for s in shapes],
        in_specs=[vmem] * len(shapes),
        out_specs=[hbm] * len(shapes),
        scratch_shapes=[dma((len(shapes),))],
        name="write_out",
    )(*[pltpu.with_memory_space_constraint(a, pltpu.VMEM) for a in held])
    return (
        gq.reshape(T, 4, D),
        gk.reshape(T, 2, D),
        gv.reshape(T, 2, D),
        gq_gain.reshape(D),
        gk_gain.reshape(D),
    )


def solution(mesh):
    split = P("seq", "head", None)
    return jax.shard_map(
        functools.partial(per_device, mesh.shape["seq"], mesh.shape["head"]),
        mesh=mesh,
        in_specs=(split, split, split, split, P(), P()),
        out_specs=(split, split, split, P(), P()),
        check_vma=False,
    )
```
